256 devices in a mesh: tm: 16 (over y_hi, z), tx: 4 (over x), ty: 4 (over y_lo, core).
Axes of the slice: x: 4, y: 4 (y_hi: 2, y_lo: 2; y = y_hi * 2 + y_lo), z: 8, core: 2. Of those that a mesh axis runs over, the one named last changes fastest.
Arguments:
- positions: float32 [16, 5, 3, 4, 4, 384], P('tm', None, None, 'tx', 'ty'), may hold values from 0 to 1
- vorticity: float32 [16, 5, 3, 4, 4, 384], P('tm', None, None, 'tx', 'ty'), may hold values from -4 to 4.4
Outputs:
- swept_positions: float32 [16, 4, 3, 4, 4, 384], P('tm', None, None, 'tx', 'ty')
- swept_vorticity: float32 [16, 4, 3, 4, 4, 384], P('tm', None, None, 'tx', 'ty')
- restart_positions: float32 [16, 3, 4, 4, 384], P('tm', None, 'tx', 'ty')
- restart_vorticity: float32 [16, 3, 4, 4, 384], P('tm', None, 'tx', 'ty')
The draws below stay inside these ranges and needn't reach their ends.
All inputs are finite; a program needn't handle non-finite values.
Results may differ from the reference program's by a relative error of at most 0.0003.
Values sent between devices are 32-bit elements; how exact they have to be, the bound alone decides.
A program may use at most 192 MiB of HBM per device.

```python
import math
import jax
import jax.numpy as jnp
from jax import lax

BLOBS = 384
NODES = 5
CHEB_XY = 6
CHEB_Z = 4
SLICES = 16
TILES_X = 4
TILES_Y = 4


def draw_vorticity(key, part):
    noise_key = jax.random.fold_in(key, 11)
    factor_key = jax.random.fold_in(key, 12)
    phase_key = jax.random.fold_in(key, 13)
    full_shape = (SLICES, NODES, 3, TILES_X, TILES_Y, BLOBS)
    tile_factor = jax.random.uniform(factor_key, (TILES_X, TILES_Y), jnp.float32, 0.7, 1.4)
    phase = jax.random.uniform(phase_key, (), jnp.float32, 0.0, 2.0 * math.pi)
    across = (jnp.arange(TILES_X, dtype=jnp.int32).astype(jnp.float32) + 0.5) * (2.0 * math.pi / TILES_X)
    wave = 1.0 + 0.4 * jnp.sin(across + phase)
    noise = jnp.clip(jax.random.normal(noise_key, full_shape, jnp.float32), -4.0, 4.0)
    level = 0.15
    mean_y = level * wave[:, None] * tile_factor
    component = (jnp.arange(3, dtype=jnp.int32) == 1).astype(jnp.float32)
    return noise + component[None, None, :, None, None, None] * mean_y[None, None, None, :, :, None]


def steps_of(own_key, shape, cuts, low, largest):
    def one(dim, shards_of):
        steps = jax.random.uniform(jax.random.fold_in(jax.random.fold_in(own_key, 6), dim), (shards_of,), jnp.float32, low / len(cuts), largest / len(cuts))
        return jnp.repeat(jnp.exp(steps), shape[dim] // shards_of).reshape((-1,) + (1,) * (len(shape) - dim - 1))

    loudness = one(*cuts[0])
    for cut in cuts[1:]:
        loudness = loudness * one(*cut)
    return loudness


def setup_inputs(seed: int = 0) -> dict:
    splits = jax.random.split(jax.random.key(seed), 3)
    positions = jnp.clip(1.0 * jax.random.uniform(splits[0], (SLICES, NODES, 3, TILES_X, TILES_Y, BLOBS), jnp.float32) ** steps_of(splits[0], (SLICES, NODES, 3, TILES_X, TILES_Y, BLOBS), ((0, 16), (3, 4), (4, 4)), -0.2, 0.2), 0.0, 1.0)
    vorticity = draw_vorticity(jax.random.fold_in(splits[2], 71), 0)
    return dict(positions=positions, vorticity=vorticity)


core_radius = 0.15
blob_volume = 0.04
slice_step = 0.1

def lagrange_integral(node_times, which, lower, upper):
    coeffs = [1.0]
    for i in range(len(node_times)):
        if i == which:
            continue
        scale = 1.0 / (node_times[which] - node_times[i])
        grown = [0.0] * (len(coeffs) + 1)
        for k in range(len(coeffs)):
            grown[k + 1] += coeffs[k] * scale
            grown[k] -= node_times[i] * coeffs[k] * scale
        coeffs = grown
    total = 0.0
    for k in range(len(coeffs)):
        upper_power = 1.0
        lower_power = 1.0
        for step in range(k + 1):
            upper_power = upper_power * upper
            lower_power = lower_power * lower
        total += coeffs[k] * (upper_power - lower_power) / (k + 1)
    return total

def collocation_tables():
    spread_root = math.sqrt(3.0 / 7.0)
    node_times = [0.0, 0.5 - 0.5 * spread_root, 0.5, 0.5 + 0.5 * spread_root, 1.0]
    weight_table = []
    for m in range(4):
        weight_table.append([lagrange_integral(node_times, j, node_times[m], node_times[m + 1]) for j in range(5)])
    widths = [node_times[m + 1] - node_times[m] for m in range(4)]
    return (weight_table, widths)

def chebyshev_points(count):
    angles = (2.0 * jnp.arange(count, dtype=jnp.int32).astype(jnp.float32) + 1.0) * (math.pi / (2 * count))
    return 0.5 * (jnp.cos(angles) + 1.0)

def chebyshev_basis(coord, count):
    xi_value = 2.0 * coord - 1.0
    first_kind = [jnp.ones_like(xi_value), xi_value]
    second_kind = [jnp.ones_like(xi_value), 2.0 * xi_value]
    for l in range(2, count):
        first_kind.append(2.0 * xi_value * first_kind[-1] - first_kind[-2])
        second_kind.append(2.0 * xi_value * second_kind[-1] - second_kind[-2])
    values = []
    slopes = []
    for k in range(count):
        node_angle = (2 * k + 1) * math.pi / (2 * count)
        weight = jnp.full_like(xi_value, 1.0 / count)
        slope = jnp.zeros_like(xi_value)
        for l in range(1, count):
            factor = math.cos(l * node_angle)
            weight = weight + 2.0 / count * factor * first_kind[l]
            slope = slope + 4.0 / count * factor * l * second_kind[l - 1]
        values.append(weight)
        slopes.append(slope)
    return (jnp.stack(values), jnp.stack(slopes))

def outer_product(first_axis, second_axis, third_axis):
    joined = first_axis[:, None, None] * second_axis[None, :, None] * third_axis[None, None, :]
    return joined.reshape((-1,) + first_axis.shape[1:])

def tile_basis(places):
    along_x, slope_x = chebyshev_basis(places[:, 0], CHEB_XY)
    along_y, slope_y = chebyshev_basis(places[:, 1], CHEB_XY)
    along_z, slope_z = chebyshev_basis(places[:, 2], CHEB_Z)
    basis_values = outer_product(along_x, along_y, along_z)
    slopes = jnp.stack([outer_product(slope_x, along_y, along_z), outer_product(along_x, slope_y, along_z), outer_product(along_x, along_y, slope_z)])
    return (basis_values, slopes)

def kernel_rows(tile_x, tile_y, count_x, count_y):
    nodes_xy = chebyshev_points(CHEB_XY)
    nodes_z = chebyshev_points(CHEB_Z)
    grid_shape = (CHEB_XY, CHEB_XY, CHEB_Z)
    coord_x = jnp.broadcast_to(nodes_xy[:, None, None], grid_shape).reshape(-1)
    coord_y = jnp.broadcast_to(nodes_xy[None, :, None], grid_shape).reshape(-1)
    coord_z = jnp.broadcast_to(nodes_z[None, None, :], grid_shape).reshape(-1)
    tile_order = jnp.arange(count_x * count_y, dtype=jnp.int32)
    source_x = tile_order // count_y
    source_y = tile_order % count_y
    centred_x = (source_x - tile_x + count_x // 2) % count_x - count_x // 2
    centred_y = (source_y - tile_y + count_y // 2) % count_y - count_y // 2
    reach_z = (coord_z[:, None] - coord_z[None, :])[None]
    kernel_sum = jnp.zeros((count_x * count_y, 3, coord_x.shape[0], coord_x.shape[0]), jnp.float32)
    for shift_x in (-1, 0, 1):
        for shift_y in (-1, 0, 1):
            image_x = (centred_x + count_x * shift_x).astype(jnp.int32)
            image_y = (centred_y + count_y * shift_y).astype(jnp.int32)
            far_mask = ((jnp.abs(image_x) > 1) | (jnp.abs(image_y) > 1)).astype(jnp.float32)
            reach_x = (coord_x[:, None] - coord_x[None, :])[None] - image_x.astype(jnp.float32)[:, None, None]
            reach_y = (coord_y[:, None] - coord_y[None, :])[None] - image_y.astype(jnp.float32)[:, None, None]
            inverse = lax.rsqrt(reach_x * reach_x + reach_y * reach_y + reach_z * reach_z + core_radius * core_radius)
            inverse_cube = inverse * inverse * inverse * far_mask[:, None, None]
            full_z = jnp.broadcast_to(reach_z, reach_x.shape)
            kernel_sum = kernel_sum + jnp.stack([reach_x * inverse_cube, reach_y * inverse_cube, full_z * inverse_cube], axis=1)
    return kernel_sum

def pair_terms(targets, sources, strengths):
    coefficient = blob_volume / (4.0 * math.pi)
    relative = [targets[:, c, :, None] - sources[:, c, None, :] for c in range(3)]
    inverse = lax.rsqrt(relative[0] * relative[0] + relative[1] * relative[1] + relative[2] * relative[2] + core_radius * core_radius)
    inverse_cube = inverse * inverse * inverse
    inverse_fifth = inverse_cube * inverse * inverse
    strength = [strengths[:, c, None, :] for c in range(3)]
    crossed = [strength[(a + 1) % 3] * relative[(a + 2) % 3] - strength[(a + 2) % 3] * relative[(a + 1) % 3] for a in range(3)]
    velocity = jnp.stack([lax.optimization_barrier(jnp.sum(crossed[a] * inverse_cube, axis=2)) for a in range(3)], axis=1)
    weighted = [lax.optimization_barrier(jnp.sum(strength[b] * inverse_cube, axis=2)) for b in range(3)]
    gradient_rows = []
    for a in range(3):
        row_terms = []
        for e in range(3):
            term = -3.0 * lax.optimization_barrier(jnp.sum(crossed[a] * relative[e] * inverse_fifth, axis=2))
            if a != e:
                other = 3 - a - e
                parity = 1.0 if (other - a) % 3 == 1 else -1.0
                term = term + parity * weighted[other]
            row_terms.append(term)
        gradient_rows.append(jnp.stack(row_terms, axis=1))
    gradient = jnp.stack(gradient_rows, axis=1)
    return (coefficient * velocity, coefficient * gradient)

def far_terms(sums, basis_values, slopes):
    coefficient = blob_volume / (4.0 * math.pi)
    local_terms = coefficient * jnp.stack([sums[:, (a + 2) % 3, (a + 1) % 3] - sums[:, (a + 1) % 3, (a + 2) % 3] for a in range(3)], axis=1)
    velocity = jnp.einsum('kam,mkj->kaj', local_terms, basis_values, precision=lax.Precision.HIGHEST)
    gradient = jnp.einsum('kam,emkj->kaej', local_terms, slopes, precision=lax.Precision.HIGHEST)
    return (velocity, gradient)

def strain_rate(gradient, vortices):
    return lax.optimization_barrier(jnp.sum(gradient * vortices[:, None], axis=2))

def quadrature(values, row_terms):
    return slice_step * sum((row_terms[j] * values[j] for j in range(len(row_terms))))

def sweep(places, vortices, evaluate):
    weight_table, widths = collocation_tables()
    old_velocity, old_gradient = evaluate(places, vortices)
    old_strain = strain_rate(old_gradient, vortices)
    here_places = places[0]
    here_vortices = vortices[0]
    new_places = []
    new_vortices = []
    for m in range(4):
        if m > 0:
            velocity, gradient = evaluate(here_places[None], here_vortices[None])
            strain = strain_rate(gradient, here_vortices[None])
            next_places = here_places + slice_step * widths[m] * (velocity[0] - old_velocity[m]) + quadrature(old_velocity, weight_table[m])
            next_vortices = here_vortices + slice_step * widths[m] * (strain[0] - old_strain[m]) + quadrature(old_strain, weight_table[m])
        else:
            next_places = here_places + quadrature(old_velocity, weight_table[0])
            next_vortices = here_vortices + quadrature(old_strain, weight_table[0])
        new_places.append(next_places)
        new_vortices.append(next_vortices)
        here_places = next_places
        here_vortices = next_vortices
    return (jnp.stack(new_places), jnp.stack(new_vortices), old_gradient[0])

def evaluate_all(places, vortices, kernel_table):
    node_count = places.shape[0]
    tile_count = TILES_X * TILES_Y
    flat_places = places.reshape(node_count, 3, tile_count, BLOBS)
    flat_vortices = vortices.reshape(node_count, 3, tile_count, BLOBS)
    tiles = jnp.arange(tile_count, dtype=jnp.int32)

    def tile_moments(tile):
        here_places = lax.dynamic_index_in_dim(flat_places, tile, 2, keepdims=False)
        here_vortices = lax.dynamic_index_in_dim(flat_vortices, tile, 2, keepdims=False)
        basis_values, slopes = tile_basis(here_places)
        return jnp.einsum('nkj,kbj->kbn', basis_values, here_vortices, precision=lax.Precision.HIGHEST)
    all_moments = lax.map(tile_moments, tiles)

    def per_target(tile):
        here_places = lax.dynamic_index_in_dim(flat_places, tile, 2, keepdims=False)
        tile_x = tile // TILES_Y
        tile_y = tile % TILES_Y
        near_velocity = jnp.zeros_like(here_places)
        near_gradient = jnp.zeros(here_places.shape[:2] + (3,) + here_places.shape[2:], jnp.float32)
        for i in range(3):
            for j in range(3):
                neighbour = ((tile_x + i - 1) % TILES_X * TILES_Y + (tile_y + j - 1) % TILES_Y).astype(jnp.int32)
                offset = jnp.array([i - 1.0, j - 1.0, 0.0], jnp.float32)[None, :, None]
                sources = lax.dynamic_index_in_dim(flat_places, neighbour, 2, keepdims=False) + offset
                strengths = lax.dynamic_index_in_dim(flat_vortices, neighbour, 2, keepdims=False)
                part_velocity, part_gradient = pair_terms(here_places, sources, strengths)
                near_velocity = near_velocity + part_velocity
                near_gradient = near_gradient + part_gradient
        kernel_part = lax.dynamic_index_in_dim(kernel_table, tile, 0, keepdims=False)
        sums = jnp.einsum('rcmn,rkbn->kcbm', kernel_part, all_moments, precision=lax.Precision.HIGHEST)
        basis_values, slopes = tile_basis(here_places)
        far_velocity, far_gradient = far_terms(sums, basis_values, slopes)
        return (near_velocity + far_velocity, near_gradient + far_gradient)
    velocity, gradient = lax.map(per_target, tiles)
    velocity = jnp.transpose(velocity, (1, 2, 0, 3)).reshape(node_count, 3, TILES_X, TILES_Y, BLOBS)
    gradient = jnp.transpose(gradient, (1, 2, 3, 0, 4)).reshape(node_count, 3, 3, TILES_X, TILES_Y, BLOBS)
    return (velocity, gradient)

def reference(positions, vorticity):
    tiles = jnp.arange(TILES_X * TILES_Y, dtype=jnp.int32)

    def table_row(tile):
        return kernel_rows(tile // TILES_Y, tile % TILES_Y, TILES_X, TILES_Y)
    kernel_table = lax.map(table_row, tiles)

    def evaluate(places, vortices):
        return evaluate_all(places, vortices, kernel_table)

    def slice_sweep(pieces):
        return sweep(pieces[0], pieces[1], evaluate)
    swept_places, swept_vortices, start_gradient = lax.map(slice_sweep, (positions, vorticity))
    delta_places = jnp.zeros_like(positions[0, 0])
    delta_vortices = jnp.zeros_like(vorticity[0, 0])
    restart_places = []
    restart_vortices = []
    for n in range(SLICES):
        restart_places.append(positions[n, 0] + delta_places)
        restart_vortices.append(vorticity[n, 0] + delta_vortices)
        if n + 1 < SLICES:
            mismatch_places = swept_places[n, 3] - positions[n + 1, 0]
            mismatch_vortices = swept_vortices[n, 3] - vorticity[n + 1, 0]
            spun = delta_vortices + slice_step * lax.optimization_barrier(jnp.sum(start_gradient[n] * delta_vortices[None], axis=1))
            delta_vortices = spun + mismatch_vortices
            delta_places = delta_places + mismatch_places
    return (swept_places, swept_vortices, jnp.stack(restart_places), jnp.stack(restart_vortices))
```

```python
import functools
import math

import jax
import jax.numpy as jnp
import numpy as np
from jax import lax
from jax.experimental import pallas as pl
from jax.experimental.pallas import tpu as pltpu
from jax.sharding import PartitionSpec as P

CHEB_XY = 6
CHEB_Z = 4
core_radius = 0.15
blob_volume = 0.04
slice_step = 0.1
COEFF = blob_volume / (4.0 * math.pi)
EPS2 = core_radius * core_radius

f32 = jnp.float32
bf16 = jnp.bfloat16
MESH = pl.DeviceIdType.MESH

OFFSETS = ((0, 1), (0, -1), (1, 0), (-1, 0), (1, 1), (-1, -1), (1, -1), (-1, 1))


def lagrange_integral(node_times, which, lower, upper):
    coeffs = [1.0]
    for i in range(len(node_times)):
        if i == which:
            continue
        scale = 1.0 / (node_times[which] - node_times[i])
        grown = [0.0] * (len(coeffs) + 1)
        for k in range(len(coeffs)):
            grown[k + 1] += coeffs[k] * scale
            grown[k] -= node_times[i] * coeffs[k] * scale
        coeffs = grown
    total = 0.0
    for k in range(len(coeffs)):
        total += coeffs[k] * (upper ** (k + 1) - lower ** (k + 1)) / (k + 1)
    return total


def collocation_tables():
    root = math.sqrt(3.0 / 7.0)
    times = [0.0, 0.5 - 0.5 * root, 0.5, 0.5 + 0.5 * root, 1.0]
    table = [
        [lagrange_integral(times, j, times[m], times[m + 1]) for j in range(5)] for m in range(4)
    ]
    return table, [times[m + 1] - times[m] for m in range(4)]


QUAD, WIDTHS = collocation_tables()


def np_split(value, parts):
    out, rest = [], np.asarray(value, np.float64)
    for _ in range(parts):
        piece = rest.astype(bf16)
        out.append(piece)
        rest = rest - piece.astype(np.float64)
    return out


def cheb_series(count):
    value = np.zeros((count, 6))
    slope = np.zeros((count, 6))
    for k in range(count):
        angle = (2 * k + 1) * math.pi / (2 * count)
        value[k, 0] = 1.0 / count
        for l in range(1, count):
            factor = math.cos(l * angle)
            value[k, l] = 2.0 / count * factor
            for j in range(l - 1, -1, -2):
                slope[k, j] += 4.0 / count * factor * l * (1.0 if j == 0 else 2.0)
    return value, slope


ROWS_SX, ROWS_DX, ROWS_SY, ROWS_P0, ROWS_P1 = 0, 8, 16, 24, 32
ROWS_RY, ROWS_RDY, ROWS_RE, ROWS_RDE, ROWS_ALL = 40, 72, 104, 136, 176


def basis_matrix():
    val, slo = cheb_series(CHEB_XY)
    zval, zslo = cheb_series(CHEB_Z)
    even = {
        (p, k): (zval[k] + s * zval[3 - k], zslo[k] + s * zslo[3 - k])
        for p, s in ((0, 1.0), (1, -1.0))
        for k in (0, 1)
    }
    full = np.zeros((ROWS_ALL, 6, 8))
    for k in range(CHEB_XY):
        full[ROWS_SX + k, :, 0] = val[k]
        full[ROWS_DX + k, :, 0] = slo[k]
        full[ROWS_SY + k, :, 1] = val[k]
    for p in (0, 1):
        for b in range(3):
            full[ROWS_P0 + 3 * p + b, :, 2] = even[p, 0][0]
            full[ROWS_P1 + 3 * p + b, :, 2] = even[p, 1][0]
        for ky in range(CHEB_XY):
            for kz in (0, 1):
                row = 16 * p + 2 * ky + kz
                full[ROWS_RY + row, :, 1] = val[ky]
                full[ROWS_RDY + row, :, 1] = slo[ky]
                full[ROWS_RE + row, :, 2] = even[p, kz][0]
                full[ROWS_RDE + row, :, 2] = even[p, kz][1]
    high, mid, low = np_split(full.reshape(ROWS_ALL, 48), 3)
    return np.concatenate([high, high, high, mid, mid, low], axis=1)


def far_table():
    pxy = 0.5 * (np.cos((2 * np.arange(6) + 1) * math.pi / 12) + 1)
    pz = 0.5 * (np.cos((2 * np.arange(4) + 1) * math.pi / 8) + 1)
    gx, gy, gz = (g.reshape(-1) for g in np.meshgrid(pxy, pxy, pz, indexing="ij"))
    out = np.zeros((16, 2, 96, 216))
    for ex in range(4):
        for ey in range(4):
            cx, cy = (ex + 2) % 4 - 2, (ey + 2) % 4 - 2
            total = np.zeros((3, 144, 144))
            for kx in (-1, 0, 1):
                for ky in (-1, 0, 1):
                    dx, dy = cx + 4 * kx, cy + 4 * ky
                    if abs(dx) <= 1 and abs(dy) <= 1:
                        continue
                    rx = gx[:, None] - gx[None, :] - dx
                    ry = gy[:, None] - gy[None, :] - dy
                    rz = gz[:, None] - gz[None, :]
                    cube = (rx * rx + ry * ry + rz * rz + EPS2) ** -1.5
                    total += np.stack([rx * cube, ry * cube, rz * cube])
            total = COEFF * total.reshape(3, 6, 6, 4, 6, 6, 4)
            for p, sign in ((0, 1.0), (1, -1.0)):
                part = 0.5 * (
                    total[:, :, :, :2, :, :, :2] + sign * total[:, :, :, :2, :, :, :1:-1]
                )
                part = part.transpose(6, 4, 5, 0, 1, 2, 3).reshape(2, 6, 6, 216)
                padded = np.zeros((2, 6, 8, 216))
                padded[:, :, :6] = part
                out[4 * ex + ey, p] = padded.reshape(96, 216)
    high, low = np_split(out.reshape(32, 96, 216), 2)
    both = np.zeros((32, 96, 512), bf16)
    both[:, :, :216] = high
    both[:, :, 256:472] = low
    return both


def split3(v):
    a = v.astype(bf16).astype(f32)
    r = v - a
    b = r.astype(bf16).astype(f32)
    return a, b, r - b


def split2(v):
    a = v.astype(bf16).astype(f32)
    return a, v - a


def mm(a, b):
    return jnp.dot(a, b, preferred_element_type=f32)


def row(v, k):
    return v[k : k + 1]


def cross_rows(a, b):
    return [a[(k + 1) % 3] * b[(k + 2) % 3] - a[(k + 2) % 3] * b[(k + 1) % 3] for k in range(3)]


def target_side(state):
    x = [row(state, k) - 0.5 for k in range(3)]
    z = jnp.zeros_like(x[0])
    one = jnp.ones_like(x[0])
    xv = jnp.concatenate(
        [-2.0 * x[0], -2.0 * x[1], -2.0 * x[2], one, x[0] * x[0] + x[1] * x[1] + x[2] * x[2], z, z, z],
        0,
    )
    h, m, l = split3(xv)
    return jnp.concatenate([h, m, h, m, l, h], 0).astype(bf16)


def source_side(state, ox, oy):
    y = [row(state, 0) + (ox - 0.5), row(state, 1) + (oy - 0.5), row(state, 2) - 0.5]
    w = [row(state, 3), row(state, 4), row(state, 5)]
    s = y[0] * y[0] + y[1] * y[1] + y[2] * y[2] + EPS2
    z = jnp.zeros_like(s)
    one = jnp.ones_like(s)
    yv = jnp.concatenate([y[0], y[1], y[2], s, one, z, z, z], 0)
    q = jnp.concatenate(w + cross_rows(w, y) + [z, z], 0)
    h, m, l = split3(yv)
    lhs = jnp.concatenate([h, h, m, m, h, l], 0).T.astype(bf16)
    columns = jnp.concatenate([q, q * y[0], q * y[1], q * y[2], q * s], 0)
    a, b, c = split3(columns)
    weights = jnp.concatenate([a, b, c, jnp.zeros_like(c[:8])], 0).astype(bf16)
    return lhs, weights


def near_chunk(targets, state, ox, oy):
    lhs, weights = source_side(state, ox, oy)
    inv = lax.rsqrt(mm(lhs, targets))
    i2 = inv * inv
    k5 = (i2 * i2) * inv
    kh = k5.astype(bf16)
    kl = (k5 - kh.astype(f32)).astype(bf16)
    return mm(weights, kh), mm(weights[0:80], kl)


def all_basis(state, cmat):
    keep = lax.broadcasted_iota(jnp.int32, state.shape, 0) < 3
    xi = jnp.where(keep, 2.0 * state - 1.0, 0.0)
    ts = [jnp.ones_like(xi), xi]
    for _ in range(2, 6):
        ts.append(2.0 * xi * ts[-1] - ts[-2])
    h, m, l = split3(jnp.concatenate(ts, 0))
    return mm(cmat, jnp.concatenate([h, m, l, h, m, h], 0).astype(bf16))


def moments_of(state, basis):
    sy = basis[ROWS_SY : ROWS_SY + 8]
    q = jnp.concatenate([row(basis, ROWS_SX + k) * sy for k in range(6)], 0)
    w3 = state[3:6]
    w = jnp.concatenate([w3, w3, jnp.zeros_like(state[0:2])], 0)
    p0 = basis[ROWS_P0 : ROWS_P0 + 8] * w
    p1 = basis[ROWS_P1 : ROWS_P1 + 8] * w
    lhs = jnp.concatenate([*split2(p0), *split2(p1)], 0).astype(bf16)
    pad = jnp.zeros((80, q.shape[1]), f32)
    out = sum(
        lax.dot_general(
            lhs,
            jnp.concatenate([part, pad], 0).astype(bf16),
            (((1,), (1,)), ((), ())),
            preferred_element_type=f32,
        )
        for part in split2(q)
    )
    return out[0:8] + out[8:16] + pltpu.roll(out[16:24] + out[24:32], 48, 1)


def local_rows(sums_plus, sums_minus):
    parts = {}
    for c in range(3):
        for p, sums in ((0, sums_plus), (1, sums_minus)):
            turned = sums if c == 0 else pltpu.roll(sums, 256 - 72 * c, 1)
            parts[p, c] = turned[3 * p : 3 * p + 3, 0:128]

    def local(p):
        rows = []
        for a in range(3):
            c1, c2 = (a + 2) % 3, (a + 1) % 3
            p1 = 1 - p if c1 == 2 else p
            p2 = 1 - p if c2 == 2 else p
            rows.append(row(parts[p1, c1], (a + 1) % 3) - row(parts[p2, c2], (a + 2) % 3))
        return jnp.concatenate(rows + [jnp.zeros((5, 128), f32)], 0)

    plus, minus = local(0), local(1)
    lane = lax.broadcasted_iota(jnp.int32, (8, 128), 1)
    blocks = []
    for kx in range(6):
        first = plus if kx == 0 else pltpu.roll(plus, 128 - 12 * kx, 1)
        second = pltpu.roll(minus, (128 + 16 - 12 * kx) % 128, 1)
        blocks.append(
            jnp.where(
                lane < 12, first, jnp.where((lane >= 16) & (lane < 28), second, 0.0)
            )
        )
    h, l = split2(jnp.concatenate(blocks, 0))
    return jnp.concatenate([h, l], 0).astype(bf16)[:, 0:32]


def far_products(local, basis):
    sy = basis[ROWS_RY : ROWS_RY + 32]
    dy = basis[ROWS_RDY : ROWS_RDY + 32]
    e = basis[ROWS_RE : ROWS_RE + 32]
    de = basis[ROWS_RDE : ROWS_RDE + 32]
    found = []
    for r in (sy * e, dy * e, sy * de):
        h, l = split2(r)
        top = mm(local, h.astype(bf16))
        found.append(top[0:48] + top[48:96] + mm(local[0:48], l.astype(bf16)))
    return found


def weighted_blocks(basis, first, blocks):
    return sum(row(basis, first + k) * blocks[8 * k : 8 * k + 8] for k in range(6))


def near_parts(state, high, low):
    s = (high[0:40] + (high[40:80] + high[80:120])) + (low[0:40] + low[40:80])
    s = [s[8 * k : 8 * k + 8] for k in range(5)]
    x = [row(state, k) - 0.5 for k in range(3)]
    square = x[0] * x[0] + x[1] * x[1] + x[2] * x[2]
    cube = square * s[0] - 2.0 * (x[0] * s[1] + x[1] * s[2] + x[2] * s[3]) + s[4]
    return s, x, cube


def turned(z, x):
    pieces = cross_rows([row(z, k) for k in range(3)], x)
    return [pieces[k] - row(z, 3 + k) for k in range(3)]


def tendency(state, high, low, local, basis):
    s, x, cube = near_parts(state, high, low)
    w = [row(state, 3 + k) for k in range(3)]
    d0, dy, dz = far_products(local, basis)
    far_u = weighted_blocks(basis, ROWS_SX, d0)
    far_g = weighted_blocks(basis, ROWS_SX, dy * w[1] + dz * w[2]) + w[0] * weighted_blocks(
        basis, ROWS_DX, d0
    )
    near_u = turned(cube, x)
    spin = cross_rows([row(cube, k) for k in range(3)], w)
    along = w[0] * x[0] + w[1] * x[1] + w[2] * x[2]
    mixed = along * s[0] - (w[0] * s[1] + w[1] * s[2] + w[2] * s[3])
    stretch = turned(mixed, x)
    u = [COEFF * near_u[k] + row(far_u, k) for k in range(3)]
    g = [COEFF * (spin[k] - 3.0 * stretch[k]) + row(far_g, k) for k in range(3)]
    z = jnp.zeros_like(u[0])
    return jnp.concatenate(u + g + [z, z], 0)


def gradient_columns(state, high, low, local, basis):
    s, x, cube = near_parts(state, high, low)
    d0, dy, dz = far_products(local, basis)
    far = (
        weighted_blocks(basis, ROWS_DX, d0),
        weighted_blocks(basis, ROWS_SX, dy),
        weighted_blocks(basis, ROWS_SX, dz),
    )
    base = turned(s[0], x)
    rows = []
    for e in range(3):
        moved = turned(s[1 + e], x)
        for a in range(3):
            value = -3.0 * (x[e] * base[a] - moved[a])
            if a != e:
                other = 3 - a - e
                sign = 1.0 if (other - a) % 3 == 1 else -1.0
                value = value + sign * row(cube, other)
            value = slice_step * (COEFF * value + row(far[e], a))
            rows.append(value + 1.0 if a == e else value)
    return jnp.concatenate(rows, 0)


def choose(index, values):
    out = jnp.float32(values[-1])
    for k in range(len(values) - 2, -1, -1):
        out = jnp.where(index == k, jnp.float32(values[k]), out)
    return out


def kernel(
    start_ref,
    cmat_ref,
    table_hbm,
    sp_ref,
    sv_ref,
    rp_ref,
    rv_ref,
    table,
    rim0,
    rim,
    mine,
    mom0,
    mom,
    mine_mom0,
    mine_mom,
    basis,
    acch,
    accl,
    far_sums,
    rates,
    coarse,
    coarse_all,
    gap,
    gap_all,
    following,
    drift,
    table_sem,
    rim_send,
    rim_recv,
    mom_send,
    mom_recv,
    next_send,
    next_recv,
    coarse_send,
    coarse_recv,
    gap_send,
    gap_recv,
):
    n_tm, n_x, n_y = (lax.axis_size(a) for a in ("tm", "tx", "ty"))
    tm, tx, ty = (lax.axis_index(a) for a in ("tm", "tx", "ty"))

    def tile(dx, dy):
        return {"tm": tm, "tx": lax.rem(tx + dx + n_x, n_x), "ty": lax.rem(ty + dy + n_y, n_y)}

    def slice_of(k):
        return {"tm": k, "tx": tx, "ty": ty}

    def remote(src, dst, send, recv, device):
        return pltpu.make_async_remote_copy(
            src_ref=src, dst_ref=dst, send_sem=send, recv_sem=recv, device_id=device, device_id_type=MESH
        )

    barrier = pltpu.get_barrier_semaphore()
    for ex in range(4):
        for ey in range(4):
            if ex or ey:
                pl.semaphore_signal(barrier, inc=1, device_id=tile(ex, ey), device_id_type=MESH)

    def greet(j, _):
        pl.semaphore_signal(
            barrier, inc=1, device_id=slice_of(lax.rem(tm + j, n_tm)), device_id_type=MESH
        )
        return 0

    lax.fori_loop(1, n_tm, greet, 0)
    fetch = pltpu.make_async_copy(table_hbm, table, table_sem)
    fetch.start()

    def rim_copy(src, rims, m, o):
        dx, dy = OFFSETS[o]
        return remote(src, rims.at[o ^ 1], rim_send.at[m, o], rim_recv.at[m, o ^ 1], tile(dx, dy))

    def mom_copy(src, moms, m, e):
        return remote(src, moms.at[e], mom_send.at[m, e], mom_recv.at[m, e], tile(-(e // 4), -(e % 4)))

    def own(k, _):
        state = start_ref[k]
        found = all_basis(state, cmat_ref[...])
        basis[k] = found
        mine_mom0[pl.ds(pl.multiple_of(8 * k, 8), 8)] = moments_of(state, found)
        high, low = near_chunk(target_side(state), state, 0.0, 0.0)
        acch[k] = high
        accl[k] = low
        return 0

    lax.fori_loop(0, 5, own, 0)
    pl.semaphore_wait(barrier, n_x * n_y - 1 + n_tm - 1)
    for o in range(8):
        rim_copy(start_ref, rim0, 0, o).start()

    @pl.when(tm > 0)
    def _():
        remote(start_ref.at[0], following, next_send, next_recv, slice_of(tm - 1)).start()

    for e in range(1, 16):
        mom_copy(mine_mom0, mom0, 0, e).start()

    def around(o, _):
        remote(
            start_ref, rim0.at[o], rim_send.at[0, o], rim_recv.at[0, o], tile(0, 0)
        ).wait_recv()
        ox = choose(o, [d[0] for d in OFFSETS])
        oy = choose(o, [d[1] for d in OFFSETS])
        for k in range(5):
            high, low = near_chunk(target_side(start_ref[k]), rim0[o, k], ox, oy)
            acch[k] += high
            accl[k] += low
        return 0

    lax.fori_loop(0, 8, around, 0)
    fetch.wait()
    for e in range(1, 16):
        mom_copy(mine_mom0, mom0, 0, e).wait_recv()
    mom0[0] = mine_mom0[...]

    def far_of(moms, rows):
        def one(e, _):
            h, l = split2(moms(e))
            lhs = jnp.concatenate([h, l], 0).astype(bf16)[:, 0:96]
            for p in range(2):
                out = mm(lhs, table[2 * e + p])
                out = out[:, 0:256] + out[:, 256:512]
                far_sums[p, 0:rows] += out[0:rows] + out[rows : 2 * rows]
            return 0

        far_sums[:, 0:rows] = jnp.zeros((2, rows, 256), f32)
        lax.fori_loop(0, 16, one, 0, unroll=4)

    far_of(lambda e: mom0[e], 40)

    def finish(k, _):
        state = start_ref[k]
        at = pl.ds(pl.multiple_of(8 * k, 8), 8)
        local = local_rows(far_sums[0, at], far_sums[1, at])
        rates[k] = tendency(state, acch[k], accl[k], local, basis[k])

        @pl.when(k == 0)
        def _():
            coarse[...] = gradient_columns(state, acch[k], accl[k], local, basis[k])

        return 0

    lax.fori_loop(0, 5, finish, 0)

    def later(j, _):
        @pl.when(tm + j < n_tm)
        def _():
            remote(
                coarse, coarse_all.at[tm], coarse_send.at[j], coarse_recv.at[tm], slice_of(tm + j)
            ).start()

        return 0

    lax.fori_loop(1, n_tm, later, 0)

    here = start_ref[0] + slice_step * sum(QUAD[0][j] * rates[j] for j in range(5))
    mine[0] = here
    sp_ref[0] = here[0:3]
    sv_ref[0] = here[3:6]

    def step(m, _):
        state_ref = mine.at[m - 1]
        for o in range(8):
            rim_copy(state_ref, rim.at[m - 1], m, o).start()
        state = state_ref[...]
        found = all_basis(state, cmat_ref[...])
        basis[0] = found
        mine_mom[m - 1] = moments_of(state, found)
        for e in range(1, 16):
            mom_copy(mine_mom.at[m - 1], mom.at[m - 1], m, e).start()
        targets = target_side(state)
        high, low = near_chunk(targets, state, 0.0, 0.0)
        acch[0] = high
        accl[0] = low
        for first, last in ((0, 4), (4, 8)):
            for o in range(first, last):
                rim_copy(state_ref, rim.at[m - 1], m, o ^ 1).wait_recv()
            for o in range(first, last):
                high, low = near_chunk(
                    targets, rim[m - 1, o], float(OFFSETS[o][0]), float(OFFSETS[o][1])
                )
                acch[0] += high
                accl[0] += low
        for e in range(1, 16):
            mom_copy(mine_mom.at[m - 1], mom.at[m - 1], m, e).wait_recv()
        mom[m - 1, 0] = mine_mom[m - 1]
        far_of(lambda e: mom[m - 1, e], 8)
        local = local_rows(far_sums[0, 0:8], far_sums[1, 0:8])
        rate = tendency(state, acch[0], accl[0], local, found)
        width = choose(m, [0.0, *(slice_step * WIDTHS[k] for k in (1, 2, 3))])
        total = state + width * rate
        for j in range(5):
            weight = choose(
                m,
                [0.0]
                + [
                    slice_step * (QUAD[k][j] - (WIDTHS[k] if j == k else 0.0)) for k in (1, 2, 3)
                ],
            )
            total = total + weight * rates[j]
        mine[m] = total
        sp_ref[m] = total[0:3]
        sv_ref[m] = total[3:6]
        return 0

    lax.fori_loop(1, 4, step, 0)

    @pl.when(tm < n_tm - 1)
    def _():
        remote(start_ref.at[0], following, next_send, next_recv, slice_of(tm)).wait_recv()
        gap[...] = mine[3] - following[...]

    def send_gap(j, _):
        @pl.when(tm + j < n_tm)
        def _():
            remote(gap, gap_all.at[tm], gap_send.at[j], gap_recv.at[tm], slice_of(tm + j)).start()

        return 0

    lax.fori_loop(1, n_tm, send_gap, 0)
    drift[...] = jnp.zeros_like(drift)

    def carry(k, _):
        @pl.when(k < tm)
        def _():
            remote(coarse, coarse_all.at[k], coarse_send.at[0], coarse_recv.at[k], slice_of(tm)).wait_recv()
            remote(gap, gap_all.at[k], gap_send.at[0], gap_recv.at[k], slice_of(tm)).wait_recv()
            d = drift[...]
            g = gap_all[k]
            a = coarse_all[k]
            spun = g[3:6] + (
                a[0:3] * row(d, 3) + a[3:6] * row(d, 4) + a[6:9] * row(d, 5)
            )
            drift[0:3] = d[0:3] + g[0:3]
            drift[3:6] = spun

        return 0

    lax.fori_loop(0, n_tm - 1, carry, 0)
    restart = start_ref[0] + drift[...]
    rp_ref[...] = restart[0:3]
    rv_ref[...] = restart[3:6]

    for o in range(8):
        rim_copy(start_ref, rim0, 0, o).wait_send()
    for e in range(1, 16):
        mom_copy(mine_mom0, mom0, 0, e).wait_send()

    def left(m, _):
        for o in range(8):
            rim_copy(mine.at[m - 1], rim.at[m - 1], m, o).wait_send()
        for e in range(1, 16):
            mom_copy(mine_mom.at[m - 1], mom.at[m - 1], m, e).wait_send()
        return 0

    lax.fori_loop(1, 4, left, 0)

    @pl.when(tm > 0)
    def _():
        remote(start_ref.at[0], following, next_send, next_recv, slice_of(tm - 1)).wait_send()

    def gone(j, _):
        @pl.when(tm + j < n_tm)
        def _():
            remote(coarse, coarse_all.at[0], coarse_send.at[j], coarse_recv.at[0], slice_of(tm)).wait_send()
            remote(gap, gap_all.at[0], gap_send.at[j], gap_recv.at[0], slice_of(tm)).wait_send()

        return 0

    lax.fori_loop(1, n_tm, gone, 0)


def local(cmat, table, positions, vorticity):
    nodes, blobs = positions.shape[1], positions.shape[-1]
    n_tm = lax.axis_size("tm")
    places = positions.reshape(nodes, 3, blobs)
    vortices = vorticity.reshape(nodes, 3, blobs)
    start = jnp.concatenate([places, vortices, jnp.zeros((nodes, 2, blobs), f32)], axis=1)
    vmem = pl.BlockSpec(memory_space=pltpu.VMEM)
    dma = pltpu.SemaphoreType.DMA
    sp, sv, rp, rv = pl.pallas_call(
        kernel,
        out_shape=(
            jax.ShapeDtypeStruct((4, 3, blobs), f32),
            jax.ShapeDtypeStruct((4, 3, blobs), f32),
            jax.ShapeDtypeStruct((3, blobs), f32),
            jax.ShapeDtypeStruct((3, blobs), f32),
        ),
        in_specs=[vmem, vmem, pl.BlockSpec(memory_space=pl.ANY)],
        out_specs=[vmem] * 4,
        scratch_shapes=[
            pltpu.VMEM((32, 96, 512), bf16),
            pltpu.VMEM((8, 5, 8, blobs), f32),
            pltpu.VMEM((3, 8, 8, blobs), f32),
            pltpu.VMEM((4, 8, blobs), f32),
            pltpu.VMEM((16, 40, 128), f32),
            pltpu.VMEM((3, 16, 8, 128), f32),
            pltpu.VMEM((40, 128), f32),
            pltpu.VMEM((3, 8, 128), f32),
            pltpu.VMEM((5, ROWS_ALL, blobs), f32),
            pltpu.VMEM((5, 128, blobs), f32),
            pltpu.VMEM((5, 80, blobs), f32),
            pltpu.VMEM((2, 40, 256), f32),
            pltpu.VMEM((5, 8, blobs), f32),
            pltpu.VMEM((9, blobs), f32),
            pltpu.VMEM((n_tm, 9, blobs), f32),
            pltpu.VMEM((8, blobs), f32),
            pltpu.VMEM((n_tm, 8, blobs), f32),
            pltpu.VMEM((8, blobs), f32),
            pltpu.VMEM((8, blobs), f32),
            dma,
            dma((4, 8)),
            dma((4, 8)),
            dma((4, 16)),
            dma((4, 16)),
            dma,
            dma,
            dma((n_tm,)),
            dma((n_tm,)),
            dma((n_tm,)),
            dma((n_tm,)),
        ],
        compiler_params=pltpu.CompilerParams(collective_id=0, has_side_effects=True),
        name="iteration",
    )(start, jnp.asarray(cmat), jnp.asarray(table))
    return (
        sp.reshape(1, 4, 3, 1, 1, blobs),
        sv.reshape(1, 4, 3, 1, 1, blobs),
        rp.reshape(1, 3, 1, 1, blobs),
        rv.reshape(1, 3, 1, 1, blobs),
    )


def solution(mesh):
    return jax.shard_map(
        functools.partial(local, basis_matrix(), far_table()),
        mesh=mesh,
        in_specs=(P("tm", None, None, "tx", "ty", None), P("tm", None, None, "tx", "ty", None)),
        out_specs=(
            P("tm", None, None, "tx", "ty", None),
            P("tm", None, None, "tx", "ty", None),
            P("tm", None, "tx", "ty", None),
            P("tm", None, "tx", "ty", None),
        ),
        check_vma=False,
    )
```

```python
import functools
import math

import jax
import jax.numpy as jnp
import numpy as np
from jax import lax
from jax.experimental import pallas as pl
from jax.experimental.pallas import tpu as pltpu
from jax.sharding import PartitionSpec as P

CHEB_XY = 6
CHEB_Z = 4
core_radius = 0.15
blob_volume = 0.04
slice_step = 0.1
COEFF = blob_volume / (4.0 * math.pi)
EPS2 = core_radius * core_radius

f32 = jnp.float32
bf16 = jnp.bfloat16
MESH = pl.DeviceIdType.MESH

OFFSETS = ((0, 1), (0, -1), (1, 0), (-1, 0), (1, 1), (-1, -1), (1, -1), (-1, 1))


SOURCES = (10, 9, 11, 8, 5, 7, 6, 13, 15, 14, 4, 12, 2, 1, 3)


def lagrange_integral(node_times, which, lower, upper):
    coeffs = [1.0]
    for i in range(len(node_times)):
        if i == which:
            continue
        scale = 1.0 / (node_times[which] - node_times[i])
        grown = [0.0] * (len(coeffs) + 1)
        for k in range(len(coeffs)):
            grown[k + 1] += coeffs[k] * scale
            grown[k] -= node_times[i] * coeffs[k] * scale
        coeffs = grown
    total = 0.0
    for k in range(len(coeffs)):
        total += coeffs[k] * (upper ** (k + 1) - lower ** (k + 1)) / (k + 1)
    return total


def collocation_tables():
    root = math.sqrt(3.0 / 7.0)
    times = [0.0, 0.5 - 0.5 * root, 0.5, 0.5 + 0.5 * root, 1.0]
    table = [
        [lagrange_integral(times, j, times[m], times[m + 1]) for j in range(5)] for m in range(4)
    ]
    return table, [times[m + 1] - times[m] for m in range(4)]


QUAD, WIDTHS = collocation_tables()


def np_split(value, parts):
    out, rest = [], np.asarray(value, np.float64)
    for _ in range(parts):
        piece = rest.astype(bf16)
        out.append(piece)
        rest = rest - piece.astype(np.float64)
    return out


def cheb_series(count):
    value = np.zeros((count, 6))
    slope = np.zeros((count, 6))
    for k in range(count):
        angle = (2 * k + 1) * math.pi / (2 * count)
        value[k, 0] = 1.0 / count
        for l in range(1, count):
            factor = math.cos(l * angle)
            value[k, l] = 2.0 / count * factor
            for j in range(l - 1, -1, -2):
                slope[k, j] += 4.0 / count * factor * l * (1.0 if j == 0 else 2.0)
    return value, slope


ROWS_SX, ROWS_DX, ROWS_P0, ROWS_P1 = 0, 8, 16, 24
ROWS_RY, ROWS_RDY, ROWS_RE, ROWS_RDE = 32, 64, 96, 128
ROWS_QX, ROWS_QY, ROWS_ALL = 160, 200, 240


def basis_matrix():
    val, slo = cheb_series(CHEB_XY)
    zval, zslo = cheb_series(CHEB_Z)
    even = {
        (p, k): (zval[k] + s * zval[3 - k], zslo[k] + s * zslo[3 - k])
        for p, s in ((0, 1.0), (1, -1.0))
        for k in (0, 1)
    }
    full = np.zeros((ROWS_ALL, 6, 8))
    for k in range(CHEB_XY):
        full[ROWS_SX + k, :, 0] = val[k]
        full[ROWS_DX + k, :, 0] = slo[k]
        for j in range(CHEB_XY):
            full[ROWS_QX + 6 * k + j, :, 0] = val[k]
            full[ROWS_QY + 6 * k + j, :, 1] = val[j]
    for p in (0, 1):
        for b in range(3):
            full[ROWS_P0 + 3 * p + b, :, 2] = even[p, 0][0]
            full[ROWS_P1 + 3 * p + b, :, 2] = even[p, 1][0]
        for ky in range(CHEB_XY):
            for kz in (0, 1):
                row = 16 * p + 2 * ky + kz
                full[ROWS_RY + row, :, 1] = val[ky]
                full[ROWS_RDY + row, :, 1] = slo[ky]
                full[ROWS_RE + row, :, 2] = even[p, kz][0]
                full[ROWS_RDE + row, :, 2] = even[p, kz][1]
    high, mid, low = np_split(full.reshape(ROWS_ALL, 48), 3)
    return np.concatenate([high, high, high, mid, mid, low], axis=1)


def far_table():
    pxy = 0.5 * (np.cos((2 * np.arange(6) + 1) * math.pi / 12) + 1)
    pz = 0.5 * (np.cos((2 * np.arange(4) + 1) * math.pi / 8) + 1)
    gx, gy, gz = (g.reshape(-1) for g in np.meshgrid(pxy, pxy, pz, indexing="ij"))
    out = np.zeros((16, 2, 80, 216))
    for ex in range(4):
        for ey in range(4):
            cx, cy = (ex + 2) % 4 - 2, (ey + 2) % 4 - 2
            total = np.zeros((3, 144, 144))
            for kx in (-1, 0, 1):
                for ky in (-1, 0, 1):
                    dx, dy = cx + 4 * kx, cy + 4 * ky
                    if abs(dx) <= 1 and abs(dy) <= 1:
                        continue
                    rx = gx[:, None] - gx[None, :] - dx
                    ry = gy[:, None] - gy[None, :] - dy
                    rz = gz[:, None] - gz[None, :]
                    cube = (rx * rx + ry * ry + rz * rz + EPS2) ** -1.5
                    total += np.stack([rx * cube, ry * cube, rz * cube])
            total = COEFF * total.reshape(3, 6, 6, 4, 6, 6, 4)
            for p, sign in ((0, 1.0), (1, -1.0)):
                part = 0.5 * (
                    total[:, :, :, :2, :, :, :2] + sign * total[:, :, :, :2, :, :, :1:-1]
                )
                out[4 * ex + ey, p, :72] = part.transpose(6, 4, 5, 0, 1, 2, 3).reshape(72, 216)
    high, low = np_split(out.reshape(32, 80, 216), 2)
    both = np.zeros((32, 80, 512), bf16)
    both[:, :, :216] = high
    both[:, :, 256:472] = low
    return both


def split3(v):
    a = v.astype(bf16).astype(f32)
    r = v - a
    b = r.astype(bf16).astype(f32)
    return a, b, r - b


def split2(v):
    a = v.astype(bf16).astype(f32)
    return a, v - a


def mm(a, b):
    return jnp.dot(a, b, preferred_element_type=f32)


def row(v, k):
    return v[k : k + 1]


def cross_rows(a, b):
    return [a[(k + 1) % 3] * b[(k + 2) % 3] - a[(k + 2) % 3] * b[(k + 1) % 3] for k in range(3)]


def target_side(state):
    x = [row(state, k) - 0.5 for k in range(3)]
    z = jnp.zeros_like(x[0])
    one = jnp.ones_like(x[0])
    xv = jnp.concatenate(
        [-2.0 * x[0], -2.0 * x[1], -2.0 * x[2], one, x[0] * x[0] + x[1] * x[1] + x[2] * x[2], z, z, z],
        0,
    )
    h, m, l = split3(xv)
    return jnp.concatenate([h, m, h, m, l, h], 0).astype(bf16)


def source_side(state, ox, oy):
    y = [row(state, 0) + (ox - 0.5), row(state, 1) + (oy - 0.5), row(state, 2) - 0.5]
    w = [row(state, 3), row(state, 4), row(state, 5)]
    s = y[0] * y[0] + y[1] * y[1] + y[2] * y[2] + EPS2
    z = jnp.zeros_like(s)
    one = jnp.ones_like(s)
    yv = jnp.concatenate([y[0], y[1], y[2], s, one, z, z, z], 0)
    q = jnp.concatenate(w + cross_rows(w, y) + [z, z], 0)
    h, m, l = split3(yv)
    lhs = jnp.concatenate([h, h, m, m, h, l], 0).T.astype(bf16)
    columns = jnp.concatenate([q, q * y[0], q * y[1], q * y[2], q * s], 0)
    a, b, c = split3(columns)
    weights = jnp.concatenate([a, b, c, jnp.zeros_like(c[:8])], 0).astype(bf16)
    return lhs, weights


def near_sums(targets, tiles):
    weights, highs, lows = [], [], []
    for state, ox, oy in tiles:
        lhs, columns = source_side(state, ox, oy)
        inv = lax.rsqrt(mm(lhs, targets))
        i2 = inv * inv
        k5 = (i2 * i2) * inv
        kh = k5.astype(bf16)
        weights.append(columns)
        highs.append(kh)
        lows.append((k5 - kh.astype(f32)).astype(bf16))
    if len(tiles) > 1:
        weights, highs, lows = (
            [jnp.concatenate(v, axis)] for v, axis in ((weights, 1), (highs, 0), (lows, 0))
        )
    return mm(weights[0], highs[0]), mm(weights[0][0:80], lows[0])


def all_basis(state, cmat):
    keep = lax.broadcasted_iota(jnp.int32, state.shape, 0) < 3
    xi = jnp.where(keep, 2.0 * state - 1.0, 0.0)
    ts = [jnp.ones_like(xi), xi]
    for _ in range(2, 6):
        ts.append(2.0 * xi * ts[-1] - ts[-2])
    h, m, l = split3(jnp.concatenate(ts, 0))
    return mm(cmat, jnp.concatenate([h, m, l, h, m, h], 0).astype(bf16))


def moments_of(state, basis):
    q = basis[ROWS_QX : ROWS_QX + 40] * basis[ROWS_QY : ROWS_QY + 40]
    w3 = state[3:6]
    w = jnp.concatenate([w3, w3, jnp.zeros_like(state[0:2])], 0)
    p0 = basis[ROWS_P0 : ROWS_P0 + 8] * w
    p1 = basis[ROWS_P1 : ROWS_P1 + 8] * w
    lhs = jnp.concatenate([*split2(p0), *split2(p1)], 0).astype(bf16)
    pad = jnp.zeros((88, q.shape[1]), f32)
    out = sum(
        lax.dot_general(
            lhs,
            jnp.concatenate([part, pad], 0).astype(bf16),
            (((1,), (1,)), ((), ())),
            preferred_element_type=f32,
        )
        for part in split2(q)
    )
    return out[0:8] + out[8:16] + pltpu.roll(out[16:24] + out[24:32], 36, 1)


def local_rows(sums_plus, sums_minus):
    parts = {}
    for c in range(3):
        for p, sums in ((0, sums_plus), (1, sums_minus)):
            turned = sums if c == 0 else pltpu.roll(sums, 256 - 72 * c, 1)
            parts[p, c] = turned[3 * p : 3 * p + 3, 0:128]

    def local(p):
        rows = []
        for a in range(3):
            c1, c2 = (a + 2) % 3, (a + 1) % 3
            p1 = 1 - p if c1 == 2 else p
            p2 = 1 - p if c2 == 2 else p
            rows.append(row(parts[p1, c1], (a + 1) % 3) - row(parts[p2, c2], (a + 2) % 3))
        return jnp.concatenate(rows + [jnp.zeros((5, 128), f32)], 0)

    plus, minus = local(0), local(1)
    lane = lax.broadcasted_iota(jnp.int32, (8, 128), 1)
    blocks = []
    for kx in range(6):
        first = plus if kx == 0 else pltpu.roll(plus, 128 - 12 * kx, 1)
        second = pltpu.roll(minus, (128 + 16 - 12 * kx) % 128, 1)
        blocks.append(
            jnp.where(
                lane < 12, first, jnp.where((lane >= 16) & (lane < 28), second, 0.0)
            )
        )
    h, l = split2(jnp.concatenate(blocks, 0))
    return jnp.concatenate([h, l], 0).astype(bf16)[:, 0:32]


def far_products(local, basis):
    sy = basis[ROWS_RY : ROWS_RY + 32]
    dy = basis[ROWS_RDY : ROWS_RDY + 32]
    e = basis[ROWS_RE : ROWS_RE + 32]
    de = basis[ROWS_RDE : ROWS_RDE + 32]
    found = []
    for r in (sy * e, dy * e, sy * de):
        h, l = split2(r)
        top = mm(local, h.astype(bf16))
        found.append(top[0:48] + top[48:96] + mm(local[0:48], l.astype(bf16)))
    return found


def weighted_blocks(basis, first, blocks):
    return sum(row(basis, first + k) * blocks[8 * k : 8 * k + 8] for k in range(6))


def near_parts(state, high, low):
    s = (high[0:40] + (high[40:80] + high[80:120])) + (low[0:40] + low[40:80])
    s = [s[8 * k : 8 * k + 8] for k in range(5)]
    x = [row(state, k) - 0.5 for k in range(3)]
    square = x[0] * x[0] + x[1] * x[1] + x[2] * x[2]
    cube = square * s[0] - 2.0 * (x[0] * s[1] + x[1] * s[2] + x[2] * s[3]) + s[4]
    return s, x, cube


def turned(z, x):
    pieces = cross_rows([row(z, k) for k in range(3)], x)
    return [pieces[k] - row(z, 3 + k) for k in range(3)]


def tendency(state, high, low, local, basis):
    s, x, cube = near_parts(state, high, low)
    w = [row(state, 3 + k) for k in range(3)]
    d0, dy, dz = far_products(local, basis)
    far_u = weighted_blocks(basis, ROWS_SX, d0)
    far_g = weighted_blocks(basis, ROWS_SX, dy * w[1] + dz * w[2]) + w[0] * weighted_blocks(
        basis, ROWS_DX, d0
    )
    near_u = turned(cube, x)
    spin = cross_rows([row(cube, k) for k in range(3)], w)
    along = w[0] * x[0] + w[1] * x[1] + w[2] * x[2]
    mixed = along * s[0] - (w[0] * s[1] + w[1] * s[2] + w[2] * s[3])
    stretch = turned(mixed, x)
    u = [COEFF * near_u[k] + row(far_u, k) for k in range(3)]
    g = [COEFF * (spin[k] - 3.0 * stretch[k]) + row(far_g, k) for k in range(3)]
    z = jnp.zeros_like(u[0])
    return jnp.concatenate(u + g + [z, z], 0)


def gradient_columns(state, high, low, local, basis):
    s, x, cube = near_parts(state, high, low)
    d0, dy, dz = far_products(local, basis)
    far = (
        weighted_blocks(basis, ROWS_DX, d0),
        weighted_blocks(basis, ROWS_SX, dy),
        weighted_blocks(basis, ROWS_SX, dz),
    )
    base = turned(s[0], x)
    rows = []
    for e in range(3):
        moved = turned(s[1 + e], x)
        for a in range(3):
            value = -3.0 * (x[e] * base[a] - moved[a])
            if a != e:
                other = 3 - a - e
                sign = 1.0 if (other - a) % 3 == 1 else -1.0
                value = value + sign * row(cube, other)
            value = slice_step * (COEFF * value + row(far[e], a))
            rows.append(value + 1.0 if a == e else value)
    return jnp.concatenate(rows, 0)


def choose(index, values):
    out = jnp.float32(values[-1])
    for k in range(len(values) - 2, -1, -1):
        out = jnp.where(index == k, jnp.float32(values[k]), out)
    return out


def far_dots(moments, table, e):
    h, l = split2(moments)
    lhs = jnp.concatenate([h, l], 0).astype(bf16)[:, 0:80]
    rows = moments.shape[0]
    found = []
    for p in range(2):
        out = mm(lhs, table[2 * e + p])
        out = out[:, 0:256] + out[:, 256:512]
        found.append(out[0:rows] + out[rows : 2 * rows])
    return found


def kernel(
    pos_hbm,
    vor_hbm,
    cmat_hbm,
    table_hbm,
    out_ref,
    pos_ref,
    vor_ref,
    cmat_ref,
    start_ref,
    table,
    rim0,
    rim,
    mine,
    mom0,
    mom,
    basis,
    sides,
    acch,
    accl,
    far_sums,
    rates,
    coarse,
    coarse_all,
    gap,
    gap_all,
    following,
    load_sem,
    rim_send,
    rim_recv0,
    rim_recv,
    mom_send,
    mom_recv0,
    mom_recv,
    next_send,
    next_recv,
    coarse_send,
    coarse_recv,
    gap_send,
    gap_recv,
    known_sem,
):
    n_tm, n_x, n_y = (lax.axis_size(a) for a in ("tm", "tx", "ty"))
    tm, tx, ty = (lax.axis_index(a) for a in ("tm", "tx", "ty"))

    def around_of(at, count):
        return [at] + [at + d - jnp.where(at + d >= count, count, 0) for d in (1, 2, 3)]

    columns, rows = around_of(tx, n_x), around_of(ty, n_y)

    def tile(dx, dy):
        return {"tm": tm, "tx": columns[dx % 4], "ty": rows[dy % 4]}

    def slice_of(k):
        return {"tm": k, "tx": tx, "ty": ty}

    def remote(src, dst, send, recv, device):
        return pltpu.make_async_remote_copy(
            src_ref=src, dst_ref=dst, send_sem=send, recv_sem=recv, device_id=device, device_id_type=MESH
        )

    barrier = pltpu.get_barrier_semaphore()

    half = n_tm // 2
    z = lax.rem(tm, half)
    partner = lax.rem(tm + half, n_tm)

    def tell(sem, distance):
        @pl.when(z + distance < half)
        def _():
            pl.semaphore_signal(
                sem, inc=1, device_id=slice_of(tm + distance), device_id_type=MESH
            )

        @pl.when(z >= distance)
        def _():
            pl.semaphore_signal(
                sem, inc=1, device_id=slice_of(tm - distance), device_id_type=MESH
            )

    def callers(distance):
        return jnp.where(z + distance < half, 1, 0) + jnp.where(z >= distance, 1, 0)

    for ex in range(4):
        for ey in range(4):
            if ex or ey:
                pl.semaphore_signal(barrier, inc=1, device_id=tile(ex, ey), device_id_type=MESH)
    tell(barrier, 1)
    pl.semaphore_signal(barrier, inc=1, device_id=slice_of(partner), device_id_type=MESH)
    def rim_copy(src, rims, m, o):
        dx, dy = OFFSETS[o]
        recv = rim_recv0.at[o // 2] if m is None else rim_recv.at[m - 1, o // 4]
        send = rim_send.at[0 if m is None else m]
        return remote(src, rims.at[o ^ 1], send, recv, tile(dx, dy))

    def mom_copy(moms, m, e):
        recv = mom_recv0.at[(e - 1) // 5] if m is None else mom_recv.at[m - 1]
        send = mom_send.at[0 if m is None else m]
        return remote(moms.at[0], moms.at[e], send, recv, tile(-(e // 4), -(e % 4)))

    def bytes_of(region, sem):
        return remote(region, region, sem, sem, tile(0, 0))

    loads = [
        pltpu.make_async_copy(src, dst, load_sem.at[i])
        for i, (src, dst) in enumerate(
            ((pos_hbm, pos_ref), (vor_hbm, vor_ref), (cmat_hbm, cmat_ref), (table_hbm, table))
        )
    ]
    for load in loads:
        load.start()
    for load in loads[:2]:
        load.wait()

    for k in range(5):
        lines = [pos_ref[3 * k + c] for c in range(3)] + [vor_ref[3 * k + c] for c in range(3)]
        start_ref[k] = jnp.concatenate(lines + [jnp.zeros_like(lines[0])] * 2, 0)
    pl.semaphore_wait(barrier, n_x * n_y + callers(1))
    for o in range(8):
        rim_copy(start_ref.at[:, 0:6], rim0.at[:, :, 0:6], None, o).start()
    tell(known_sem.at[0], 1)
    pl.semaphore_signal(known_sem.at[0], inc=1, device_id=slice_of(partner), device_id_type=MESH)
    loads[2].wait()
    for k in range(5):
        state = start_ref[k]
        found = all_basis(state, cmat_ref[...])
        basis[k] = found
        mom0[0, 6 * k : 6 * k + 6] = moments_of(state, found)[0:6]
    mom0[0, 30:32] = jnp.zeros_like(mom0[0, 30:32])
    for e in range(1, 16):
        mom_copy(mom0, None, e).start()
    far_sums[...] = jnp.zeros_like(far_sums)
    for k in range(5):
        state = start_ref[k]
        side = target_side(state)
        sides[k] = side
        acch[k], accl[k] = near_sums(side, [(state, 0.0, 0.0)])
    loads[3].wait()

    def around(i, _):
        bytes_of(rim0.at[pl.ds(2 * i, 2), :, 0:6], rim_recv0.at[i]).wait_recv()

        @pl.when(i > 0)
        def _():
            bytes_of(mom0.at[pl.ds(5 * i - 4, 5)], mom_recv0.at[i - 1]).wait_recv()

        @pl.when(i == 2)
        def _():
            pl.semaphore_wait(known_sem.at[0], callers(1) + 1)
            tell(known_sem.at[1], 2)

        scale = choose(i, [0.2, 1.0])
        sources = [(5 * i - 4 + t) * ((i + 3) // 4) for t in range(5)]
        found = [far_dots(mom0[e], table, e) for e in sources]
        for p in range(2):
            far_sums[p] += scale * sum(f[p] for f in found)
        ox, oy = choose(i, [0.0, 1.0]), choose(i, [1.0, 0.0, 1.0, -1.0])
        for k in range(5):
            high, low = near_sums(
                sides[k],
                [(rim0[2 * i, k, 0:6], ox, oy), (rim0[2 * i + 1, k, 0:6], -ox, -oy)],
            )
            acch[k] += high
            accl[k] += low
        return 0

    lax.fori_loop(0, 4, around, 0)
    pl.semaphore_wait(known_sem.at[1], callers(2))
    tell(known_sem.at[2], 4)
    for k in range(5):
        state = start_ref[k]
        local = local_rows(
            far_sums[0, 6 * k : 6 * k + 6], far_sums[1, 6 * k : 6 * k + 6]
        )
        if k == 0:
            coarse[...] = gradient_columns(state, acch[k], accl[k], local, basis[k])
        rates[k] = tendency(state, acch[k], accl[k], local, basis[k])

    here = start_ref[0] + slice_step * sum(QUAD[0][j] * rates[j] for j in range(5))
    mine[0] = here
    out_ref[0] = here

    def later(j, wide):
        gap_z = j - half
        near_by = jnp.where(z + j < half, jnp.where(j <= 4, 1, 0), jnp.where(gap_z * gap_z <= 9, 1, 0))

        @pl.when((tm + j < n_tm) & (near_by == 1 - wide))
        def _():
            remote(
                coarse, coarse_all.at[tm], coarse_send.at[j], coarse_recv.at[tm], slice_of(tm + j)
            ).start()

        return wide

    def step(m, _):
        state_ref = mine.at[m - 1, 0:6]
        rims, moms = rim.at[m - 1, :, 0:6], mom.at[m - 1]
        for o in range(8):
            rim_copy(state_ref, rims, m, o).start()
        state = mine[m - 1]
        found = all_basis(state, cmat_ref[...])
        basis[0] = found
        moms[0] = moments_of(state, found)
        sent = mom.at[m - 1, :, 0:6]
        for e in SOURCES:
            mom_copy(sent, m, e).start()
        targets = target_side(state)
        high, low = near_sums(targets, [(state, 0.0, 0.0)])
        acch[0] = high
        accl[0] = low

        def some(first, last):
            tiles = [
                (rim[m - 1, o, 0:6], float(OFFSETS[o][0]), float(OFFSETS[o][1]))
                for o in range(first, last)
            ]
            high, low = near_sums(targets, tiles)
            acch[0] += high
            accl[0] += low

        bytes_of(rim.at[m - 1, 0:4, 0:6], rim_recv.at[m - 1, 0]).wait_recv()
        some(0, 4)
        bytes_of(rim.at[m - 1, 4:8, 0:6], rim_recv.at[m - 1, 1]).wait_recv()
        some(4, 7)
        bytes_of(mom.at[m - 1, 1:16, 0:6], mom_recv.at[m - 1]).wait_recv()
        far = [far_dots(moms[e], table, e) for e in range(16)]
        some(7, 8)

        @pl.when(m == 2)
        def _():
            pl.semaphore_wait(known_sem.at[2], callers(4))

            @pl.when(tm > 0)
            def _():
                remote(start_ref.at[0], following, next_send, next_recv, slice_of(tm - 1)).start()

        @pl.when(m < 3)
        def _():
            lax.fori_loop(1, n_tm, later, m - 1)

        local = local_rows(*(sum(f[p] for f in far) for p in range(2)))
        rate = tendency(state, acch[0], accl[0], local, found)
        width = choose(m, [0.0, *(slice_step * WIDTHS[k] for k in (1, 2, 3))])
        total = state
        for j in range(5):
            weight = choose(
                m,
                [0.0]
                + [
                    slice_step * (QUAD[k][j] - (WIDTHS[k] if j == k else 0.0)) for k in (1, 2, 3)
                ],
            )
            total = total + weight * rates[j]
        total = total + width * rate
        mine[m] = total
        out_ref[m] = total
        return 0

    lax.fori_loop(1, 4, step, 0)

    @pl.when(tm < n_tm - 1)
    def _():
        remote(start_ref.at[0], following, next_send, next_recv, slice_of(tm)).wait_recv()
        gap[...] = mine[3] - following[...]

    def send_gap(j, _):
        far = n_tm - j

        @pl.when(tm + far < n_tm)
        def _():
            remote(
                gap, gap_all.at[tm], gap_send.at[far], gap_recv.at[tm], slice_of(tm + far)
            ).start()

        return 0

    lax.fori_loop(1, n_tm, send_gap, 0)

    def arrived(k, _):
        @pl.when(k < tm)
        def _():
            remote(coarse, coarse_all.at[k], coarse_send.at[0], coarse_recv.at[k], slice_of(tm)).wait_recv()
            remote(gap, gap_all.at[k], gap_send.at[0], gap_recv.at[k], slice_of(tm)).wait_recv()

        return 0

    lax.fori_loop(0, n_tm - 1, arrived, 0)
    moved = jnp.zeros((3, gap_all.shape[2]), f32)
    spun = jnp.zeros_like(moved)
    for k in range(n_tm - 1):
        g = gap_all[k]
        a = coarse_all[k]
        after = g[3:6] + (a[0:3] * row(spun, 0) + a[3:6] * row(spun, 1) + a[6:9] * row(spun, 2))
        spun = jnp.where(k < tm, after, spun)
        moved = jnp.where(k < tm, moved + g[0:3], moved)
    out_ref[4] = start_ref[0] + jnp.concatenate([moved, spun, jnp.zeros_like(moved[0:2])], 0)

    bytes_of(rim0.at[:, :, 0:6], rim_send.at[0]).wait_send()
    bytes_of(mom0.at[1:16], mom_send.at[0]).wait_send()
    for m in range(1, 4):
        bytes_of(rim.at[m - 1, :, 0:6], rim_send.at[m]).wait_send()
        bytes_of(mom.at[m - 1, 1:16, 0:6], mom_send.at[m]).wait_send()

    @pl.when(tm > 0)
    def _():
        remote(start_ref.at[0], following, next_send, next_recv, slice_of(tm - 1)).wait_send()

    def gone(j, _):
        @pl.when(tm + j < n_tm)
        def _():
            remote(coarse, coarse_all.at[0], coarse_send.at[j], coarse_recv.at[0], slice_of(tm)).wait_send()
            remote(gap, gap_all.at[0], gap_send.at[j], gap_recv.at[0], slice_of(tm)).wait_send()

        return 0

    lax.fori_loop(1, n_tm, gone, 0)


def spread(all_ref, sp_ref, sv_ref, rp_ref, rv_ref):
    for m in range(4):
        for c in range(3):
            sp_ref[3 * m + c] = all_ref[m, c : c + 1]
            sv_ref[3 * m + c] = all_ref[m, 3 + c : 4 + c]
    for c in range(3):
        rp_ref[c] = all_ref[4, c : c + 1]
        rv_ref[c] = all_ref[4, 3 + c : 4 + c]


def local(cmat, table, positions, vorticity):
    nodes, blobs = positions.shape[1], positions.shape[-1]
    n_tm = lax.axis_size("tm")
    places = positions.reshape(nodes * 3, 1, blobs)
    vortices = vorticity.reshape(nodes * 3, 1, blobs)
    vmem = pl.BlockSpec(memory_space=pltpu.VMEM)
    dma = pltpu.SemaphoreType.DMA
    everything = pl.pallas_call(
        kernel,
        out_shape=jax.ShapeDtypeStruct((5, 8, blobs), f32),
        in_specs=[pl.BlockSpec(memory_space=pl.ANY)] * 4,
        out_specs=vmem,
        scratch_shapes=[
            pltpu.VMEM((nodes * 3, 1, blobs), f32),
            pltpu.VMEM((nodes * 3, 1, blobs), f32),
            pltpu.VMEM(cmat.shape, bf16),
            pltpu.VMEM((5, 8, blobs), f32),
            pltpu.VMEM((32, 80, 512), bf16),
            pltpu.VMEM((8, 5, 8, blobs), f32),
            pltpu.VMEM((3, 8, 8, blobs), f32),
            pltpu.VMEM((4, 8, blobs), f32),
            pltpu.VMEM((16, 32, 128), f32),
            pltpu.VMEM((3, 16, 8, 128), f32),
            pltpu.VMEM((5, ROWS_ALL, blobs), f32),
            pltpu.VMEM((5, 48, blobs), bf16),
            pltpu.VMEM((5, 128, blobs), f32),
            pltpu.VMEM((5, 80, blobs), f32),
            pltpu.VMEM((2, 32, 256), f32),
            pltpu.VMEM((5, 8, blobs), f32),
            pltpu.VMEM((9, blobs), f32),
            pltpu.VMEM((n_tm, 9, blobs), f32),
            pltpu.VMEM((8, blobs), f32),
            pltpu.VMEM((n_tm, 8, blobs), f32),
            pltpu.VMEM((8, blobs), f32),
            dma((4,)),
            dma((4,)),
            dma((4,)),
            dma((3, 2)),
            dma((4,)),
            dma((3,)),
            dma((3,)),
            dma,
            dma,
            dma((n_tm,)),
            dma((n_tm,)),
            dma((n_tm,)),
            dma((n_tm,)),
            pltpu.SemaphoreType.REGULAR((3,)),
        ],
        compiler_params=pltpu.CompilerParams(collective_id=0, has_side_effects=True),
        name="iteration",
    )(places, vortices, jnp.asarray(cmat), jnp.asarray(table))
    sp, sv, rp, rv = pl.pallas_call(
        spread,
        out_shape=tuple(jax.ShapeDtypeStruct((n, 1, blobs), f32) for n in (12, 12, 3, 3)),
        in_specs=[vmem],
        out_specs=[vmem] * 4,
        name="spread",
    )(everything)
    return (
        sp.reshape(1, 4, 3, 1, 1, blobs),
        sv.reshape(1, 4, 3, 1, 1, blobs),
        rp.reshape(1, 3, 1, 1, blobs),
        rv.reshape(1, 3, 1, 1, blobs),
    )


def solution(mesh):
    return jax.shard_map(
        functools.partial(local, basis_matrix(), far_table()),
        mesh=mesh,
        in_specs=(P("tm", None, None, "tx", "ty", None), P("tm", None, None, "tx", "ty", None)),
        out_specs=(
            P("tm", None, None, "tx", "ty", None),
            P("tm", None, None, "tx", "ty", None),
            P("tm", None, "tx", "ty", None),
            P("tm", None, "tx", "ty", None),
        ),
        check_vma=False,
    )
```

```python
import functools
import math

import jax
import jax.numpy as jnp
import numpy as np
from jax import lax
from jax.experimental import pallas as pl
from jax.experimental.pallas import tpu as pltpu
from jax.sharding import PartitionSpec as P

CHEB_XY = 6
CHEB_Z = 4
core_radius = 0.15
blob_volume = 0.04
slice_step = 0.1
COEFF = blob_volume / (4.0 * math.pi)
EPS2 = core_radius * core_radius

f32 = jnp.float32
bf16 = jnp.bfloat16
MESH = pl.DeviceIdType.MESH

OFFSETS = ((0, 1), (0, -1), (1, 0), (-1, 0), (1, 1), (-1, -1), (1, -1), (-1, 1))


GROUP_OF = (0, 0, 1, 2)
SOURCES = (10, 9, 11, 8, 5, 7, 6, 13, 15, 14, 4, 12, 2, 1, 3)


def lagrange_integral(node_times, which, lower, upper):
    coeffs = [1.0]
    for i in range(len(node_times)):
        if i == which:
            continue
        scale = 1.0 / (node_times[which] - node_times[i])
        grown = [0.0] * (len(coeffs) + 1)
        for k in range(len(coeffs)):
            grown[k + 1] += coeffs[k] * scale
            grown[k] -= node_times[i] * coeffs[k] * scale
        coeffs = grown
    total = 0.0
    for k in range(len(coeffs)):
        total += coeffs[k] * (upper ** (k + 1) - lower ** (k + 1)) / (k + 1)
    return total


def collocation_tables():
    root = math.sqrt(3.0 / 7.0)
    times = [0.0, 0.5 - 0.5 * root, 0.5, 0.5 + 0.5 * root, 1.0]
    table = [
        [lagrange_integral(times, j, times[m], times[m + 1]) for j in range(5)] for m in range(4)
    ]
    return table, [times[m + 1] - times[m] for m in range(4)]


QUAD, WIDTHS = collocation_tables()


def np_split(value, parts):
    out, rest = [], np.asarray(value, np.float64)
    for _ in range(parts):
        piece = rest.astype(bf16)
        out.append(piece)
        rest = rest - piece.astype(np.float64)
    return out


def cheb_series(count):
    value = np.zeros((count, 6))
    slope = np.zeros((count, 6))
    for k in range(count):
        angle = (2 * k + 1) * math.pi / (2 * count)
        value[k, 0] = 1.0 / count
        for l in range(1, count):
            factor = math.cos(l * angle)
            value[k, l] = 2.0 / count * factor
            for j in range(l - 1, -1, -2):
                slope[k, j] += 4.0 / count * factor * l * (1.0 if j == 0 else 2.0)
    return value, slope


ROWS_P0, ROWS_P1, ROWS_QX, ROWS_QY, ROWS_MOMENTS = 0, 8, 16, 56, 96
ROWS_SX, ROWS_DX, ROWS_RY, ROWS_RDY, ROWS_RE, ROWS_RDE = 96, 104, 112, 144, 176, 208
ROWS_ALL = 240


def basis_matrix():
    val, slo = cheb_series(CHEB_XY)
    zval, zslo = cheb_series(CHEB_Z)
    even = {
        (p, k): (zval[k] + s * zval[3 - k], zslo[k] + s * zslo[3 - k])
        for p, s in ((0, 1.0), (1, -1.0))
        for k in (0, 1)
    }
    full = np.zeros((ROWS_ALL, 6, 8))
    for k in range(CHEB_XY):
        full[ROWS_SX + k, :, 0] = val[k]
        full[ROWS_DX + k, :, 0] = slo[k]
        for j in range(CHEB_XY):
            full[ROWS_QX + 6 * k + j, :, 0] = val[k]
            full[ROWS_QY + 6 * k + j, :, 1] = val[j]
    for p in (0, 1):
        for b in range(3):
            full[ROWS_P0 + 3 * p + b, :, 2] = even[p, 0][0]
            full[ROWS_P1 + 3 * p + b, :, 2] = even[p, 1][0]
        for ky in range(CHEB_XY):
            for kz in (0, 1):
                row = 16 * p + 2 * ky + kz
                full[ROWS_RY + row, :, 1] = val[ky]
                full[ROWS_RDY + row, :, 1] = slo[ky]
                full[ROWS_RE + row, :, 2] = even[p, kz][0]
                full[ROWS_RDE + row, :, 2] = even[p, kz][1]
    high, mid, low = np_split(full.reshape(ROWS_ALL, 48), 3)
    return np.concatenate([high, high, high, mid, mid, low], axis=1)


def far_table():
    pxy = 0.5 * (np.cos((2 * np.arange(6) + 1) * math.pi / 12) + 1)
    pz = 0.5 * (np.cos((2 * np.arange(4) + 1) * math.pi / 8) + 1)
    gx, gy, gz = (g.reshape(-1) for g in np.meshgrid(pxy, pxy, pz, indexing="ij"))
    out = np.zeros((16, 2, 80, 216))
    for ex in range(4):
        for ey in range(4):
            cx, cy = (ex + 2) % 4 - 2, (ey + 2) % 4 - 2
            total = np.zeros((3, 144, 144))
            for kx in (-1, 0, 1):
                for ky in (-1, 0, 1):
                    dx, dy = cx + 4 * kx, cy + 4 * ky
                    if abs(dx) <= 1 and abs(dy) <= 1:
                        continue
                    rx = gx[:, None] - gx[None, :] - dx
                    ry = gy[:, None] - gy[None, :] - dy
                    rz = gz[:, None] - gz[None, :]
                    cube = (rx * rx + ry * ry + rz * rz + EPS2) ** -1.5
                    total += np.stack([rx * cube, ry * cube, rz * cube])
            total = COEFF * total.reshape(3, 6, 6, 4, 6, 6, 4)
            for p, sign in ((0, 1.0), (1, -1.0)):
                part = 0.5 * (
                    total[:, :, :, :2, :, :, :2] + sign * total[:, :, :, :2, :, :, :1:-1]
                )
                out[4 * ex + ey, p, :72] = part.transpose(6, 4, 5, 0, 1, 2, 3).reshape(72, 216)
    high, low = np_split(out.reshape(32, 80, 216), 2)
    both = np.zeros((32, 80, 512), bf16)
    both[:, :, :216] = high
    both[:, :, 256:472] = low
    return both


def split3(v):
    a = v.astype(bf16).astype(f32)
    r = v - a
    b = r.astype(bf16).astype(f32)
    return a, b, r - b


def split2(v):
    a = v.astype(bf16).astype(f32)
    return a, v - a


def mm(a, b):
    return jnp.dot(a, b, preferred_element_type=f32)


def row(v, k):
    return v[k : k + 1]


def cross_rows(a, b):
    return [a[(k + 1) % 3] * b[(k + 2) % 3] - a[(k + 2) % 3] * b[(k + 1) % 3] for k in range(3)]


def target_side(state):
    x = [row(state, k) - 0.5 for k in range(3)]
    z = jnp.zeros_like(x[0])
    one = jnp.ones_like(x[0])
    xv = jnp.concatenate(
        [-2.0 * x[0], -2.0 * x[1], -2.0 * x[2], one, x[0] * x[0] + x[1] * x[1] + x[2] * x[2], z, z, z],
        0,
    )
    h, m, l = split3(xv)
    return jnp.concatenate([h, m, h, m, l, h], 0).astype(bf16)


def source_side(state, ox, oy):
    y = [row(state, 0) + (ox - 0.5), row(state, 1) + (oy - 0.5), row(state, 2) - 0.5]
    w = [row(state, 3), row(state, 4), row(state, 5)]
    s = y[0] * y[0] + y[1] * y[1] + y[2] * y[2] + EPS2
    z = jnp.zeros_like(s)
    one = jnp.ones_like(s)
    yv = jnp.concatenate([y[0], y[1], y[2], s, one, z, z, z], 0)
    q = jnp.concatenate(w + cross_rows(w, y) + [z, z], 0)
    h, m, l = split3(yv)
    columns = jnp.concatenate([q, q * y[0], q * y[1], q * y[2], q * s], 0)
    a, b, c = split3(columns)
    weights = jnp.concatenate([a, b, c, jnp.zeros_like(c[:8])], 0).astype(bf16)
    return [h, h, m, m, h, l], weights


def powers(square):
    inv = lax.rsqrt(square)
    i2 = inv * inv
    k5 = (i2 * i2) * inv
    kh = k5.astype(bf16)
    return kh, (k5 - kh.astype(f32)).astype(bf16)


def weighted_sums(tiles):
    weights, highs, lows = (list(v) for v in zip(*tiles))
    if len(tiles) > 1:
        weights, highs, lows = (
            [jnp.concatenate(v, axis)] for v, axis in ((weights, 1), (highs, 0), (lows, 0))
        )
    return mm(weights[0], highs[0]), mm(weights[0][0:80], lows[0])


def near_sums(targets, tiles):
    found = []
    for tile in tiles:
        pieces, weights = source_side(*tile)
        lhs = jnp.concatenate(pieces, 0).T.astype(bf16)
        found.append((weights, *powers(mm(lhs, targets))))
    return weighted_sums(found)


def near_sums_of_two(targets, first, second):
    width = targets.shape[1] // 2
    found = [], []
    for tiles in zip(first, second):
        sides = [source_side(*tile) for tile in tiles]
        lhs = jnp.concatenate(sides[0][0] + sides[1][0], 0).T.astype(bf16)
        square = mm(lhs, targets)
        for n in range(2):
            found[n].append((sides[n][1], *powers(square[:, n * width : (n + 1) * width])))
    return weighted_sums(found[0]), weighted_sums(found[1])


def chebyshev_terms(state):
    keep = lax.broadcasted_iota(jnp.int32, state.shape, 0) < 3
    xi = jnp.where(keep, 2.0 * state - 1.0, 0.0)
    ts = [jnp.ones_like(xi), xi]
    for _ in range(2, 6):
        ts.append(2.0 * xi * ts[-1] - ts[-2])
    h, m, l = split3(jnp.concatenate(ts, 0))
    return jnp.concatenate([h, m, l, h, m, h], 0).astype(bf16)


def moments_of(state, basis):
    q = basis[ROWS_QX : ROWS_QX + 40] * basis[ROWS_QY : ROWS_QY + 40]
    w3 = state[3:6]
    w = jnp.concatenate([w3, w3, jnp.zeros_like(state[0:2])], 0)
    p0 = basis[ROWS_P0 : ROWS_P0 + 8] * w
    p1 = basis[ROWS_P1 : ROWS_P1 + 8] * w
    lhs = jnp.concatenate([*split2(p0), *split2(p1)], 0).astype(bf16)
    pad = jnp.zeros((88, q.shape[1]), f32)
    out = sum(
        lax.dot_general(
            lhs,
            jnp.concatenate([part, pad], 0).astype(bf16),
            (((1,), (1,)), ((), ())),
            preferred_element_type=f32,
        )
        for part in split2(q)
    )
    return out[0:8] + out[8:16] + pltpu.roll(out[16:24] + out[24:32], 36, 1)


def local_rows(sums_plus, sums_minus):
    parts = {}
    for c in range(3):
        for p, sums in ((0, sums_plus), (1, sums_minus)):
            turned = sums if c == 0 else pltpu.roll(sums, 256 - 72 * c, 1)
            parts[p, c] = turned[3 * p : 3 * p + 3, 0:128]

    def local(p):
        rows = []
        for a in range(3):
            c1, c2 = (a + 2) % 3, (a + 1) % 3
            p1 = 1 - p if c1 == 2 else p
            p2 = 1 - p if c2 == 2 else p
            rows.append(row(parts[p1, c1], (a + 1) % 3) - row(parts[p2, c2], (a + 2) % 3))
        return jnp.concatenate(rows + [jnp.zeros((5, 128), f32)], 0)

    plus, minus = local(0), local(1)
    lane = lax.broadcasted_iota(jnp.int32, (8, 128), 1)
    blocks = []
    for kx in range(6):
        first = plus if kx == 0 else pltpu.roll(plus, 128 - 12 * kx, 1)
        second = pltpu.roll(minus, (128 + 16 - 12 * kx) % 128, 1)
        blocks.append(
            jnp.where(
                lane < 12, first, jnp.where((lane >= 16) & (lane < 28), second, 0.0)
            )
        )
    h, l = split2(jnp.concatenate(blocks, 0))
    return jnp.concatenate([h, l], 0).astype(bf16)[:, 0:32]


def far_products(local, basis):
    sy = basis[ROWS_RY : ROWS_RY + 32]
    dy = basis[ROWS_RDY : ROWS_RDY + 32]
    e = basis[ROWS_RE : ROWS_RE + 32]
    de = basis[ROWS_RDE : ROWS_RDE + 32]
    found = []
    for r in (sy * e, dy * e, sy * de):
        h, l = split2(r)
        top = mm(local, h.astype(bf16))
        found.append(top[0:48] + top[48:96] + mm(local[0:48], l.astype(bf16)))
    return found


def weighted_blocks(basis, first, blocks):
    return sum(row(basis, first + k) * blocks[8 * k : 8 * k + 8] for k in range(6))


def near_parts(state, high, low):
    s = (high[0:40] + (high[40:80] + high[80:120])) + (low[0:40] + low[40:80])
    s = [s[8 * k : 8 * k + 8] for k in range(5)]
    x = [row(state, k) - 0.5 for k in range(3)]
    square = x[0] * x[0] + x[1] * x[1] + x[2] * x[2]
    cube = square * s[0] - 2.0 * (x[0] * s[1] + x[1] * s[2] + x[2] * s[3]) + s[4]
    return s, x, cube


def turned(z, x):
    pieces = cross_rows([row(z, k) for k in range(3)], x)
    return [pieces[k] - row(z, 3 + k) for k in range(3)]


def tendency(state, high, low, local, basis):
    s, x, cube = near_parts(state, high, low)
    w = [row(state, 3 + k) for k in range(3)]
    d0, dy, dz = far_products(local, basis)
    far_u = weighted_blocks(basis, ROWS_SX, d0)
    far_g = weighted_blocks(basis, ROWS_SX, dy * w[1] + dz * w[2]) + w[0] * weighted_blocks(
        basis, ROWS_DX, d0
    )
    near_u = turned(cube, x)
    spin = cross_rows([row(cube, k) for k in range(3)], w)
    along = w[0] * x[0] + w[1] * x[1] + w[2] * x[2]
    mixed = along * s[0] - (w[0] * s[1] + w[1] * s[2] + w[2] * s[3])
    stretch = turned(mixed, x)
    u = [COEFF * near_u[k] + row(far_u, k) for k in range(3)]
    g = [COEFF * (spin[k] - 3.0 * stretch[k]) + row(far_g, k) for k in range(3)]
    z = jnp.zeros_like(u[0])
    return jnp.concatenate(u + g + [z, z], 0)


def gradient_columns(state, high, low, local, basis):
    s, x, cube = near_parts(state, high, low)
    d0, dy, dz = far_products(local, basis)
    far = (
        weighted_blocks(basis, ROWS_DX, d0),
        weighted_blocks(basis, ROWS_SX, dy),
        weighted_blocks(basis, ROWS_SX, dz),
    )
    base = turned(s[0], x)
    rows = []
    for e in range(3):
        moved = turned(s[1 + e], x)
        for a in range(3):
            value = -3.0 * (x[e] * base[a] - moved[a])
            if a != e:
                other = 3 - a - e
                sign = 1.0 if (other - a) % 3 == 1 else -1.0
                value = value + sign * row(cube, other)
            value = slice_step * (COEFF * value + row(far[e], a))
            rows.append(value + 1.0 if a == e else value)
    return jnp.concatenate(rows, 0)


def choose(index, values):
    out = jnp.float32(values[-1])
    for k in range(len(values) - 2, -1, -1):
        out = jnp.where(index == k, jnp.float32(values[k]), out)
    return out


def far_dots(moments, table, e):
    h, l = split2(moments)
    lhs = jnp.concatenate([h, l], 0).astype(bf16)[:, 0:80]
    rows = moments.shape[0]
    found = []
    for p in range(2):
        out = mm(lhs, table[2 * e + p])
        out = out[:, 0:256] + out[:, 256:512]
        found.append(out[0:rows] + out[rows : 2 * rows])
    return found


def kernel(
    pos_hbm,
    vor_hbm,
    cmat_hbm,
    table_hbm,
    out_ref,
    pos_ref,
    vor_ref,
    cmat_ref,
    start_ref,
    table,
    rim0,
    rim,
    mine,
    mom0,
    mom,
    basis,
    sides,
    sides2,
    acch,
    accl,
    far_sums,
    rates,
    coarse,
    coarse_all,
    gap,
    gap_all,
    following,
    load_sem,
    rim_send,
    rim_recv0,
    rim_recv,
    mom_send,
    mom_recv0,
    mom_recv,
    next_send,
    next_recv,
    coarse_send,
    coarse_recv,
    gap_send,
    gap_recv,
    known_sem,
):
    n_tm, n_x, n_y = (lax.axis_size(a) for a in ("tm", "tx", "ty"))
    tm, tx, ty = (lax.axis_index(a) for a in ("tm", "tx", "ty"))

    def around_of(at, count):
        return [at] + [at + d - jnp.where(at + d >= count, count, 0) for d in (1, 2, 3)]

    columns, rows = around_of(tx, n_x), around_of(ty, n_y)

    def tile(dx, dy):
        return {"tm": tm, "tx": columns[dx % 4], "ty": rows[dy % 4]}

    def slice_of(k):
        return {"tm": k, "tx": tx, "ty": ty}

    def remote(src, dst, send, recv, device):
        return pltpu.make_async_remote_copy(
            src_ref=src, dst_ref=dst, send_sem=send, recv_sem=recv, device_id=device, device_id_type=MESH
        )

    barrier = pltpu.get_barrier_semaphore()

    half = n_tm // 2
    z = lax.rem(tm, half)
    partner = lax.rem(tm + half, n_tm)

    def tell(sem, distance):
        @pl.when(z + distance < half)
        def _():
            pl.semaphore_signal(
                sem, inc=1, device_id=slice_of(tm + distance), device_id_type=MESH
            )

        @pl.when(z >= distance)
        def _():
            pl.semaphore_signal(
                sem, inc=1, device_id=slice_of(tm - distance), device_id_type=MESH
            )

    def callers(distance):
        return jnp.where(z + distance < half, 1, 0) + jnp.where(z >= distance, 1, 0)

    for ex in range(4):
        for ey in range(4):
            if ex or ey:
                pl.semaphore_signal(barrier, inc=1, device_id=tile(ex, ey), device_id_type=MESH)
    tell(barrier, 1)
    pl.semaphore_signal(barrier, inc=1, device_id=slice_of(partner), device_id_type=MESH)
    def rim_copy(src, rims, m, o):
        dx, dy = OFFSETS[o]
        recv = rim_recv0.at[o // 2] if m is None else rim_recv.at[m - 1, o // 4]
        send = rim_send.at[0 if m is None else m]
        return remote(src, rims.at[o ^ 1], send, recv, tile(dx, dy))

    def mom_copy(moms, m, e):
        recv = mom_recv0.at[(e - 1) // 5] if m is None else mom_recv.at[m - 1, GROUP_OF[e // 4]]
        send = mom_send.at[0 if m is None else m]
        return remote(moms.at[0], moms.at[e], send, recv, tile(-(e // 4), -(e % 4)))

    def bytes_of(region, sem):
        return remote(region, region, sem, sem, tile(0, 0))

    loads = [
        pltpu.make_async_copy(src, dst, load_sem.at[i])
        for i, (src, dst) in enumerate(
            ((pos_hbm, pos_ref), (vor_hbm, vor_ref), (cmat_hbm, cmat_ref), (table_hbm, table))
        )
    ]
    for load in loads:
        load.start()
    for load in loads[:2]:
        load.wait()

    for k in range(5):
        lines = [pos_ref[3 * k + c] for c in range(3)] + [vor_ref[3 * k + c] for c in range(3)]
        start_ref[k] = jnp.concatenate(lines + [jnp.zeros_like(lines[0])] * 2, 0)
    pl.semaphore_wait(barrier, n_x * n_y + callers(1))
    for o in range(8):
        rim_copy(start_ref.at[:, 0:6], rim0.at[:, :, 0:6], None, o).start()
    tell(known_sem.at[0], 1)
    pl.semaphore_signal(known_sem.at[0], inc=1, device_id=slice_of(partner), device_id_type=MESH)
    loads[2].wait()
    for k in range(5):
        state = start_ref[k]
        found = mm(cmat_ref[...], chebyshev_terms(state))
        basis[k] = found
        mom0[0, 6 * k : 6 * k + 6] = moments_of(state, found)[0:6]
    mom0[0, 30:32] = jnp.zeros_like(mom0[0, 30:32])
    for e in range(1, 16):
        mom_copy(mom0, None, e).start()
    far_sums[...] = jnp.zeros_like(far_sums)
    for k in range(5):
        state = start_ref[k]
        side = target_side(state)
        if k < 4:
            width = side.shape[1]
            at = 48 * (k % 2)
            sides2[k // 2, at : at + 48, width * (k % 2) : width * (k % 2 + 1)] = side
            sides2[k // 2, at : at + 48, width * (1 - k % 2) : width * (2 - k % 2)] = jnp.zeros_like(side)
        else:
            sides[...] = side
        acch[k], accl[k] = near_sums(side, [(state, 0.0, 0.0)])
    loads[3].wait()

    def around(i, _):
        bytes_of(rim0.at[pl.ds(2 * i, 2), :, 0:6], rim_recv0.at[i]).wait_recv()

        @pl.when(i > 0)
        def _():
            bytes_of(mom0.at[pl.ds(5 * i - 4, 5)], mom_recv0.at[i - 1]).wait_recv()

        @pl.when(i == 2)
        def _():
            pl.semaphore_wait(known_sem.at[0], callers(1) + 1)
            tell(known_sem.at[1], 2)

        scale = choose(i, [0.2, 1.0])
        sources = [(5 * i - 4 + t) * ((i + 3) // 4) for t in range(5)]
        found = [far_dots(mom0[e], table, e) for e in sources]
        for p in range(2):
            far_sums[p] += scale * sum(f[p] for f in found)
        ox, oy = choose(i, [0.0, 1.0]), choose(i, [1.0, 0.0, 1.0, -1.0])

        def both(k):
            return [(rim0[2 * i, k, 0:6], ox, oy), (rim0[2 * i + 1, k, 0:6], -ox, -oy)]

        for k in (0, 2):
            pair = near_sums_of_two(sides2[k // 2], both(k), both(k + 1))
            for n in range(2):
                acch[k + n] += pair[n][0]
                accl[k + n] += pair[n][1]
        high, low = near_sums(sides[...], both(4))
        acch[4] += high
        accl[4] += low
        return 0

    lax.fori_loop(0, 4, around, 0)
    pl.semaphore_wait(known_sem.at[1], callers(2))
    tell(known_sem.at[2], 4)
    for k in range(5):
        state = start_ref[k]
        local = local_rows(
            far_sums[0, 6 * k : 6 * k + 6], far_sums[1, 6 * k : 6 * k + 6]
        )
        if k == 0:
            coarse[...] = gradient_columns(state, acch[k], accl[k], local, basis[k])
        rates[k] = tendency(state, acch[k], accl[k], local, basis[k])

    here = start_ref[0] + slice_step * sum(QUAD[0][j] * rates[j] for j in range(5))
    mine[0] = here
    out_ref[0] = here

    def later(j, wide):
        gap_z = j - half
        near_by = jnp.where(z + j < half, jnp.where(j <= 4, 1, 0), jnp.where(gap_z * gap_z <= 9, 1, 0))

        @pl.when((tm + j < n_tm) & (near_by == 1 - wide))
        def _():
            remote(
                coarse, coarse_all.at[tm], coarse_send.at[j], coarse_recv.at[tm], slice_of(tm + j)
            ).start()

        return wide

    def step(m, _):
        state_ref = mine.at[m - 1, 0:6]
        rims, moms = rim.at[m - 1, :, 0:6], mom.at[m - 1]
        for o in range(8):
            rim_copy(state_ref, rims, m, o).start()
        state = mine[m - 1]
        terms = chebyshev_terms(state)
        moms[0] = moments_of(state, mm(cmat_ref[0:ROWS_MOMENTS], terms))
        sent = mom.at[m - 1, :, 0:6]
        for e in SOURCES:
            mom_copy(sent, m, e).start()
        basis[0, ROWS_MOMENTS:ROWS_ALL] = mm(cmat_ref[ROWS_MOMENTS:ROWS_ALL], terms)
        targets = target_side(state)
        high, low = near_sums(targets, [(state, 0.0, 0.0)])
        acch[0] = high
        accl[0] = low

        def some(first, last):
            tiles = [
                (rim[m - 1, o, 0:6], float(OFFSETS[o][0]), float(OFFSETS[o][1]))
                for o in range(first, last)
            ]
            high, low = near_sums(targets, tiles)
            acch[0] += high
            accl[0] += low

        bytes_of(rim.at[m - 1, 0:4, 0:6], rim_recv.at[m - 1, 0]).wait_recv()
        some(0, 4)
        bytes_of(rim.at[m - 1, 4:8, 0:6], rim_recv.at[m - 1, 1]).wait_recv()
        bytes_of(mom.at[m - 1, 1:8, 0:6], mom_recv.at[m - 1, 0]).wait_recv()
        bytes_of(mom.at[m - 1, 12:16, 0:6], mom_recv.at[m - 1, 2]).wait_recv()
        far = [far_dots(moms[e], table, e) for e in (*range(8), *range(12, 16))]
        for p in range(2):
            far_sums[p, 0:8] = sum(f[p] for f in far)
        some(4, 8)
        bytes_of(mom.at[m - 1, 8:12, 0:6], mom_recv.at[m - 1, 1]).wait_recv()
        far = [far_dots(moms[e], table, e) for e in range(8, 12)]

        @pl.when(m == 2)
        def _():
            pl.semaphore_wait(known_sem.at[2], callers(4))

            @pl.when(tm > 0)
            def _():
                remote(start_ref.at[0], following, next_send, next_recv, slice_of(tm - 1)).start()

        @pl.when(m < 3)
        def _():
            lax.fori_loop(1, n_tm, later, m - 1)

        local = local_rows(*(far_sums[p, 0:8] + sum(f[p] for f in far) for p in range(2)))
        rate = tendency(state, acch[0], accl[0], local, basis[0])
        width = choose(m, [0.0, *(slice_step * WIDTHS[k] for k in (1, 2, 3))])
        total = state
        for j in range(5):
            weight = choose(
                m,
                [0.0]
                + [
                    slice_step * (QUAD[k][j] - (WIDTHS[k] if j == k else 0.0)) for k in (1, 2, 3)
                ],
            )
            total = total + weight * rates[j]
        total = total + width * rate
        mine[m] = total
        out_ref[m] = total
        return 0

    lax.fori_loop(1, 4, step, 0)

    @pl.when(tm < n_tm - 1)
    def _():
        remote(start_ref.at[0], following, next_send, next_recv, slice_of(tm)).wait_recv()
        gap[...] = mine[3] - following[...]

    def send_gap(j, _):
        far = n_tm - j

        @pl.when(tm + far < n_tm)
        def _():
            remote(
                gap, gap_all.at[tm], gap_send.at[far], gap_recv.at[tm], slice_of(tm + far)
            ).start()

        return 0

    lax.fori_loop(1, n_tm, send_gap, 0)

    def arrived(k, _):
        @pl.when(k < tm)
        def _():
            remote(coarse, coarse_all.at[k], coarse_send.at[0], coarse_recv.at[k], slice_of(tm)).wait_recv()
            remote(gap, gap_all.at[k], gap_send.at[0], gap_recv.at[k], slice_of(tm)).wait_recv()

        return 0

    lax.fori_loop(0, n_tm - 1, arrived, 0)
    moved = jnp.zeros((3, gap_all.shape[2]), f32)
    spun = jnp.zeros_like(moved)
    for k in range(n_tm - 1):
        g = gap_all[k]
        a = coarse_all[k]
        after = g[3:6] + (a[0:3] * row(spun, 0) + a[3:6] * row(spun, 1) + a[6:9] * row(spun, 2))
        spun = jnp.where(k < tm, after, spun)
        moved = jnp.where(k < tm, moved + g[0:3], moved)
    out_ref[4] = start_ref[0] + jnp.concatenate([moved, spun, jnp.zeros_like(moved[0:2])], 0)

    bytes_of(rim0.at[:, :, 0:6], rim_send.at[0]).wait_send()
    bytes_of(mom0.at[1:16], mom_send.at[0]).wait_send()
    for m in range(1, 4):
        bytes_of(rim.at[m - 1, :, 0:6], rim_send.at[m]).wait_send()
        bytes_of(mom.at[m - 1, 1:16, 0:6], mom_send.at[m]).wait_send()

    @pl.when(tm > 0)
    def _():
        remote(start_ref.at[0], following, next_send, next_recv, slice_of(tm - 1)).wait_send()

    def gone(j, _):
        @pl.when(tm + j < n_tm)
        def _():
            remote(coarse, coarse_all.at[0], coarse_send.at[j], coarse_recv.at[0], slice_of(tm)).wait_send()
            remote(gap, gap_all.at[0], gap_send.at[j], gap_recv.at[0], slice_of(tm)).wait_send()

        return 0

    lax.fori_loop(1, n_tm, gone, 0)


def spread(all_ref, sp_ref, sv_ref, rp_ref, rv_ref):
    for m in range(4):
        for c in range(3):
            sp_ref[3 * m + c] = all_ref[m, c : c + 1]
            sv_ref[3 * m + c] = all_ref[m, 3 + c : 4 + c]
    for c in range(3):
        rp_ref[c] = all_ref[4, c : c + 1]
        rv_ref[c] = all_ref[4, 3 + c : 4 + c]


def local(cmat, table, positions, vorticity):
    nodes, blobs = positions.shape[1], positions.shape[-1]
    n_tm = lax.axis_size("tm")
    places = positions.reshape(nodes * 3, 1, blobs)
    vortices = vorticity.reshape(nodes * 3, 1, blobs)
    vmem = pl.BlockSpec(memory_space=pltpu.VMEM)
    dma = pltpu.SemaphoreType.DMA
    everything = pl.pallas_call(
        kernel,
        out_shape=jax.ShapeDtypeStruct((5, 8, blobs), f32),
        in_specs=[pl.BlockSpec(memory_space=pl.ANY)] * 4,
        out_specs=vmem,
        scratch_shapes=[
            pltpu.VMEM((nodes * 3, 1, blobs), f32),
            pltpu.VMEM((nodes * 3, 1, blobs), f32),
            pltpu.VMEM(cmat.shape, bf16),
            pltpu.VMEM((5, 8, blobs), f32),
            pltpu.VMEM((32, 80, 512), bf16),
            pltpu.VMEM((8, 5, 8, blobs), f32),
            pltpu.VMEM((3, 8, 8, blobs), f32),
            pltpu.VMEM((4, 8, blobs), f32),
            pltpu.VMEM((16, 32, 128), f32),
            pltpu.VMEM((3, 16, 8, 128), f32),
            pltpu.VMEM((5, ROWS_ALL, blobs), f32),
            pltpu.VMEM((48, blobs), bf16),
            pltpu.VMEM((2, 96, 2 * blobs), bf16),
            pltpu.VMEM((5, 128, blobs), f32),
            pltpu.VMEM((5, 80, blobs), f32),
            pltpu.VMEM((2, 32, 256), f32),
            pltpu.VMEM((5, 8, blobs), f32),
            pltpu.VMEM((9, blobs), f32),
            pltpu.VMEM((n_tm, 9, blobs), f32),
            pltpu.VMEM((8, blobs), f32),
            pltpu.VMEM((n_tm, 8, blobs), f32),
            pltpu.VMEM((8, blobs), f32),
            dma((4,)),
            dma((4,)),
            dma((4,)),
            dma((3, 2)),
            dma((4,)),
            dma((3,)),
            dma((3, 3)),
            dma,
            dma,
            dma((n_tm,)),
            dma((n_tm,)),
            dma((n_tm,)),
            dma((n_tm,)),
            pltpu.SemaphoreType.REGULAR((3,)),
        ],
        compiler_params=pltpu.CompilerParams(collective_id=0, has_side_effects=True),
        name="iteration",
    )(places, vortices, jnp.asarray(cmat), jnp.asarray(table))
    sp, sv, rp, rv = pl.pallas_call(
        spread,
        out_shape=tuple(jax.ShapeDtypeStruct((n, 1, blobs), f32) for n in (12, 12, 3, 3)),
        in_specs=[vmem],
        out_specs=[vmem] * 4,
        name="spread",
    )(everything)
    return (
        sp.reshape(1, 4, 3, 1, 1, blobs),
        sv.reshape(1, 4, 3, 1, 1, blobs),
        rp.reshape(1, 3, 1, 1, blobs),
        rv.reshape(1, 3, 1, 1, blobs),
    )


def solution(mesh):
    return jax.shard_map(
        functools.partial(local, basis_matrix(), far_table()),
        mesh=mesh,
        in_specs=(P("tm", None, None, "tx", "ty", None), P("tm", None, None, "tx", "ty", None)),
        out_specs=(
            P("tm", None, None, "tx", "ty", None),
            P("tm", None, None, "tx", "ty", None),
            P("tm", None, "tx", "ty", None),
            P("tm", None, "tx", "ty", None),
        ),
        check_vma=False,
    )
```

```python
import functools
import math

import jax
import jax.numpy as jnp
import numpy as np
from jax import lax
from jax.experimental import pallas as pl
from jax.experimental.pallas import tpu as pltpu
from jax.sharding import PartitionSpec as P

CHEB_XY = 6
CHEB_Z = 4
core_radius = 0.15
blob_volume = 0.04
slice_step = 0.1
COEFF = blob_volume / (4.0 * math.pi)
EPS2 = core_radius * core_radius

f32 = jnp.float32
bf16 = jnp.bfloat16
MESH = pl.DeviceIdType.MESH

OFFSETS = ((0, 1), (0, -1), (1, 0), (-1, 0), (1, 1), (-1, -1), (1, -1), (-1, 1))


GROUP_OF = (0, 0, 1, 2)
SOURCES = (10, 9, 11, 8, 5, 7, 6, 13, 15, 14, 4, 12, 2, 1, 3)


def lagrange_integral(node_times, which, lower, upper):
    coeffs = [1.0]
    for i in range(len(node_times)):
        if i == which:
            continue
        scale = 1.0 / (node_times[which] - node_times[i])
        grown = [0.0] * (len(coeffs) + 1)
        for k in range(len(coeffs)):
            grown[k + 1] += coeffs[k] * scale
            grown[k] -= node_times[i] * coeffs[k] * scale
        coeffs = grown
    total = 0.0
    for k in range(len(coeffs)):
        total += coeffs[k] * (upper ** (k + 1) - lower ** (k + 1)) / (k + 1)
    return total


def collocation_tables():
    root = math.sqrt(3.0 / 7.0)
    times = [0.0, 0.5 - 0.5 * root, 0.5, 0.5 + 0.5 * root, 1.0]
    table = [
        [lagrange_integral(times, j, times[m], times[m + 1]) for j in range(5)] for m in range(4)
    ]
    return table, [times[m + 1] - times[m] for m in range(4)]


QUAD, WIDTHS = collocation_tables()


def np_split(value, parts):
    out, rest = [], np.asarray(value, np.float64)
    for _ in range(parts):
        piece = rest.astype(bf16)
        out.append(piece)
        rest = rest - piece.astype(np.float64)
    return out


def cheb_series(count):
    value = np.zeros((count, 6))
    slope = np.zeros((count, 6))
    for k in range(count):
        angle = (2 * k + 1) * math.pi / (2 * count)
        value[k, 0] = 1.0 / count
        for l in range(1, count):
            factor = math.cos(l * angle)
            value[k, l] = 2.0 / count * factor
            for j in range(l - 1, -1, -2):
                slope[k, j] += 4.0 / count * factor * l * (1.0 if j == 0 else 2.0)
    return value, slope


ROWS_P0, ROWS_P1, ROWS_QX, ROWS_QY, ROWS_MOMENTS = 0, 8, 16, 56, 96
ROWS_SX, ROWS_DX, ROWS_RY, ROWS_RDY, ROWS_RE, ROWS_RDE = 96, 104, 112, 144, 176, 208
ROWS_ALL = 240


def basis_matrix():
    val, slo = cheb_series(CHEB_XY)
    zval, zslo = cheb_series(CHEB_Z)
    even = {
        (p, k): (zval[k] + s * zval[3 - k], zslo[k] + s * zslo[3 - k])
        for p, s in ((0, 1.0), (1, -1.0))
        for k in (0, 1)
    }
    full = np.zeros((ROWS_ALL, 6, 8))
    for k in range(CHEB_XY):
        full[ROWS_SX + k, :, 0] = val[k]
        full[ROWS_DX + k, :, 0] = slo[k]
        for j in range(CHEB_XY):
            full[ROWS_QX + 6 * k + j, :, 0] = val[k]
            full[ROWS_QY + 6 * k + j, :, 1] = val[j]
    for p in (0, 1):
        for b in range(3):
            full[ROWS_P0 + 3 * p + b, :, 2] = even[p, 0][0]
            full[ROWS_P1 + 3 * p + b, :, 2] = even[p, 1][0]
        for ky in range(CHEB_XY):
            for kz in (0, 1):
                row = 16 * p + 2 * ky + kz
                full[ROWS_RY + row, :, 1] = val[ky]
                full[ROWS_RDY + row, :, 1] = slo[ky]
                full[ROWS_RE + row, :, 2] = even[p, kz][0]
                full[ROWS_RDE + row, :, 2] = even[p, kz][1]
    high, mid, low = np_split(full.reshape(ROWS_ALL, 48), 3)
    return np.concatenate([high, high, high, mid, mid, low], axis=1)


def far_table():
    pxy = 0.5 * (np.cos((2 * np.arange(6) + 1) * math.pi / 12) + 1)
    pz = 0.5 * (np.cos((2 * np.arange(4) + 1) * math.pi / 8) + 1)
    gx, gy, gz = (g.reshape(-1) for g in np.meshgrid(pxy, pxy, pz, indexing="ij"))
    out = np.zeros((16, 2, 80, 216))
    for ex in range(4):
        for ey in range(4):
            cx, cy = (ex + 2) % 4 - 2, (ey + 2) % 4 - 2
            total = np.zeros((3, 144, 144))
            for kx in (-1, 0, 1):
                for ky in (-1, 0, 1):
                    dx, dy = cx + 4 * kx, cy + 4 * ky
                    if abs(dx) <= 1 and abs(dy) <= 1:
                        continue
                    rx = gx[:, None] - gx[None, :] - dx
                    ry = gy[:, None] - gy[None, :] - dy
                    rz = gz[:, None] - gz[None, :]
                    cube = (rx * rx + ry * ry + rz * rz + EPS2) ** -1.5
                    total += np.stack([rx * cube, ry * cube, rz * cube])
            total = COEFF * total.reshape(3, 6, 6, 4, 6, 6, 4)
            for p, sign in ((0, 1.0), (1, -1.0)):
                part = 0.5 * (
                    total[:, :, :, :2, :, :, :2] + sign * total[:, :, :, :2, :, :, :1:-1]
                )
                out[4 * ex + ey, p, :72] = part.transpose(6, 4, 5, 0, 1, 2, 3).reshape(72, 216)
    high, low = np_split(out.reshape(32, 80, 216), 2)
    both = np.zeros((32, 80, 512), bf16)
    both[:, :, :216] = high
    both[:, :, 256:472] = low
    return both


def split3(v):
    a = v.astype(bf16).astype(f32)
    r = v - a
    b = r.astype(bf16).astype(f32)
    return a, b, r - b


def split2(v):
    a = v.astype(bf16).astype(f32)
    return a, v - a


def mm(a, b):
    return jnp.dot(a, b, preferred_element_type=f32)


def row(v, k):
    return v[k : k + 1]


def cross_rows(a, b):
    return [a[(k + 1) % 3] * b[(k + 2) % 3] - a[(k + 2) % 3] * b[(k + 1) % 3] for k in range(3)]


def target_side(state):
    x = [row(state, k) - 0.5 for k in range(3)]
    z = jnp.zeros_like(x[0])
    one = jnp.ones_like(x[0])
    xv = jnp.concatenate(
        [-2.0 * x[0], -2.0 * x[1], -2.0 * x[2], one, x[0] * x[0] + x[1] * x[1] + x[2] * x[2], z, z, z],
        0,
    )
    h, m, l = split3(xv)
    return jnp.concatenate([h, m, h, m, l, h], 0).astype(bf16)


def source_side(state, ox, oy):
    y = [row(state, 0) + (ox - 0.5), row(state, 1) + (oy - 0.5), row(state, 2) - 0.5]
    w = [row(state, 3), row(state, 4), row(state, 5)]
    s = y[0] * y[0] + y[1] * y[1] + y[2] * y[2] + EPS2
    z = jnp.zeros_like(s)
    one = jnp.ones_like(s)
    yv = jnp.concatenate([y[0], y[1], y[2], s, one, z, z, z], 0)
    q = jnp.concatenate(w + cross_rows(w, y) + [z, z], 0)
    h, m, l = split3(yv)
    columns = jnp.concatenate([q, q * y[0], q * y[1], q * y[2], q * s], 0)
    a, b, c = split3(columns)
    weights = jnp.concatenate([a, b, c, jnp.zeros_like(c[:8])], 0).astype(bf16)
    return [h, h, m, m, h, l], weights


def powers(square):
    inv = lax.rsqrt(square)
    i2 = inv * inv
    k5 = (i2 * i2) * inv
    kh = k5.astype(bf16)
    return kh, (k5 - kh.astype(f32)).astype(bf16)


def weighted_sums(tiles):
    weights, highs, lows = (list(v) for v in zip(*tiles))
    if len(tiles) > 1:
        weights, highs, lows = (
            [jnp.concatenate(v, axis)] for v, axis in ((weights, 1), (highs, 0), (lows, 0))
        )
    return mm(weights[0], highs[0]), mm(weights[0][0:80], lows[0])


def near_sums(targets, tiles):
    found = []
    for tile in tiles:
        pieces, weights = source_side(*tile)
        lhs = jnp.concatenate(pieces, 0).T.astype(bf16)
        found.append((weights, *powers(mm(lhs, targets))))
    return weighted_sums(found)


def near_sums_of_two(targets, first, second):
    width = targets.shape[1] // 2
    found = [], []
    for tiles in zip(first, second):
        sides = [source_side(*tile) for tile in tiles]
        lhs = jnp.concatenate(sides[0][0] + sides[1][0], 0).T.astype(bf16)
        square = mm(lhs, targets)
        for n in range(2):
            found[n].append((sides[n][1], *powers(square[:, n * width : (n + 1) * width])))
    return weighted_sums(found[0]), weighted_sums(found[1])


def chebyshev_terms(state):
    keep = lax.broadcasted_iota(jnp.int32, state.shape, 0) < 3
    xi = jnp.where(keep, 2.0 * state - 1.0, 0.0)
    ts = [jnp.ones_like(xi), xi]
    for _ in range(2, 6):
        ts.append(2.0 * xi * ts[-1] - ts[-2])
    h, m, l = split3(jnp.concatenate(ts, 0))
    return jnp.concatenate([h, m, l, h, m, h], 0).astype(bf16)


def moments_of(state, basis):
    q = basis[ROWS_QX : ROWS_QX + 40] * basis[ROWS_QY : ROWS_QY + 40]
    w3 = state[3:6]
    w = jnp.concatenate([w3, w3, jnp.zeros_like(state[0:2])], 0)
    p0 = basis[ROWS_P0 : ROWS_P0 + 8] * w
    p1 = basis[ROWS_P1 : ROWS_P1 + 8] * w
    lhs = jnp.concatenate([*split2(p0), *split2(p1)], 0).astype(bf16)
    pad = jnp.zeros((88, q.shape[1]), f32)
    out = sum(
        lax.dot_general(
            lhs,
            jnp.concatenate([part, pad], 0).astype(bf16),
            (((1,), (1,)), ((), ())),
            preferred_element_type=f32,
        )
        for part in split2(q)
    )
    return out[0:8] + out[8:16] + pltpu.roll(out[16:24] + out[24:32], 36, 1)


def local_rows(sums_plus, sums_minus):
    parts = {}
    for c in range(3):
        for p, sums in ((0, sums_plus), (1, sums_minus)):
            turned = sums if c == 0 else pltpu.roll(sums, 256 - 72 * c, 1)
            parts[p, c] = turned[3 * p : 3 * p + 3, 0:128]

    def local(p):
        rows = []
        for a in range(3):
            c1, c2 = (a + 2) % 3, (a + 1) % 3
            p1 = 1 - p if c1 == 2 else p
            p2 = 1 - p if c2 == 2 else p
            rows.append(row(parts[p1, c1], (a + 1) % 3) - row(parts[p2, c2], (a + 2) % 3))
        return jnp.concatenate(rows + [jnp.zeros((5, 128), f32)], 0)

    plus, minus = local(0), local(1)
    lane = lax.broadcasted_iota(jnp.int32, (8, 128), 1)
    blocks = []
    for kx in range(6):
        first = plus if kx == 0 else pltpu.roll(plus, 128 - 12 * kx, 1)
        second = pltpu.roll(minus, (128 + 16 - 12 * kx) % 128, 1)
        blocks.append(
            jnp.where(
                lane < 12, first, jnp.where((lane >= 16) & (lane < 28), second, 0.0)
            )
        )
    h, l = split2(jnp.concatenate(blocks, 0))
    return jnp.concatenate([h, l], 0).astype(bf16)[:, 0:32]


def far_products(local, basis):
    sy = basis[ROWS_RY : ROWS_RY + 32]
    dy = basis[ROWS_RDY : ROWS_RDY + 32]
    e = basis[ROWS_RE : ROWS_RE + 32]
    de = basis[ROWS_RDE : ROWS_RDE + 32]
    found = []
    for r in (sy * e, dy * e, sy * de):
        h, l = split2(r)
        top = mm(local, h.astype(bf16))
        found.append(top[0:48] + top[48:96] + mm(local[0:48], l.astype(bf16)))
    return found


def weighted_blocks(basis, first, blocks):
    return sum(row(basis, first + k) * blocks[8 * k : 8 * k + 8] for k in range(6))


def near_parts(state, high, low):
    s = (high[0:40] + (high[40:80] + high[80:120])) + (low[0:40] + low[40:80])
    s = [s[8 * k : 8 * k + 8] for k in range(5)]
    x = [row(state, k) - 0.5 for k in range(3)]
    square = x[0] * x[0] + x[1] * x[1] + x[2] * x[2]
    cube = square * s[0] - 2.0 * (x[0] * s[1] + x[1] * s[2] + x[2] * s[3]) + s[4]
    return s, x, cube


def turned(z, x):
    pieces = cross_rows([row(z, k) for k in range(3)], x)
    return [pieces[k] - row(z, 3 + k) for k in range(3)]


def tendency(state, high, low, local, basis):
    s, x, cube = near_parts(state, high, low)
    w = [row(state, 3 + k) for k in range(3)]
    d0, dy, dz = far_products(local, basis)
    far_u = weighted_blocks(basis, ROWS_SX, d0)
    far_g = weighted_blocks(basis, ROWS_SX, dy * w[1] + dz * w[2]) + w[0] * weighted_blocks(
        basis, ROWS_DX, d0
    )
    near_u = turned(cube, x)
    spin = cross_rows([row(cube, k) for k in range(3)], w)
    along = w[0] * x[0] + w[1] * x[1] + w[2] * x[2]
    mixed = along * s[0] - (w[0] * s[1] + w[1] * s[2] + w[2] * s[3])
    stretch = turned(mixed, x)
    u = [COEFF * near_u[k] + row(far_u, k) for k in range(3)]
    g = [COEFF * (spin[k] - 3.0 * stretch[k]) + row(far_g, k) for k in range(3)]
    z = jnp.zeros_like(u[0])
    return jnp.concatenate(u + g + [z, z], 0)


def gradient_columns(state, high, low, local, basis):
    s, x, cube = near_parts(state, high, low)
    d0, dy, dz = far_products(local, basis)
    far = (
        weighted_blocks(basis, ROWS_DX, d0),
        weighted_blocks(basis, ROWS_SX, dy),
        weighted_blocks(basis, ROWS_SX, dz),
    )
    base = turned(s[0], x)
    rows = []
    for e in range(3):
        moved = turned(s[1 + e], x)
        for a in range(3):
            value = -3.0 * (x[e] * base[a] - moved[a])
            if a != e:
                other = 3 - a - e
                sign = 1.0 if (other - a) % 3 == 1 else -1.0
                value = value + sign * row(cube, other)
            value = slice_step * (COEFF * value + row(far[e], a))
            rows.append(value + 1.0 if a == e else value)
    return jnp.concatenate(rows, 0)


def choose(index, values):
    out = jnp.float32(values[-1])
    for k in range(len(values) - 2, -1, -1):
        out = jnp.where(index == k, jnp.float32(values[k]), out)
    return out


def far_dots(moments, table, e):
    h, l = split2(moments)
    lhs = jnp.concatenate([h, l], 0).astype(bf16)[:, 0:80]
    rows = moments.shape[0]
    found = []
    for p in range(2):
        out = mm(lhs, table[2 * e + p])
        out = out[:, 0:256] + out[:, 256:512]
        found.append(out[0:rows] + out[rows : 2 * rows])
    return found


def kernel(
    pos_hbm,
    vor_hbm,
    cmat_hbm,
    table_hbm,
    out_ref,
    pos_ref,
    vor_ref,
    cmat_ref,
    start_ref,
    table,
    rim0,
    rim,
    mine,
    mom0,
    mom,
    basis,
    sides,
    sides2,
    acch,
    accl,
    far_sums,
    rates,
    coarse,
    coarse_all,
    gap,
    gap_all,
    following,
    load_sem,
    rim_send,
    rim_recv0,
    rim_recv,
    mom_send,
    mom_recv0,
    mom_recv,
    next_send,
    next_recv,
    coarse_send,
    coarse_recv,
    gap_send,
    gap_recv,
    known_sem,
):
    n_tm, n_x, n_y = (lax.axis_size(a) for a in ("tm", "tx", "ty"))
    tm, tx, ty = (lax.axis_index(a) for a in ("tm", "tx", "ty"))

    def around_of(at, count):
        return [at] + [at + d - jnp.where(at + d >= count, count, 0) for d in (1, 2, 3)]

    columns, rows = around_of(tx, n_x), around_of(ty, n_y)

    def tile(dx, dy):
        return {"tm": tm, "tx": columns[dx % 4], "ty": rows[dy % 4]}

    def slice_of(k):
        return {"tm": k, "tx": tx, "ty": ty}

    def remote(src, dst, send, recv, device):
        return pltpu.make_async_remote_copy(
            src_ref=src, dst_ref=dst, send_sem=send, recv_sem=recv, device_id=device, device_id_type=MESH
        )

    barrier = pltpu.get_barrier_semaphore()

    half = n_tm // 2
    z = lax.rem(tm, half)
    partner = lax.rem(tm + half, n_tm)

    def tell(sem, distance):
        @pl.when(z + distance < half)
        def _():
            pl.semaphore_signal(
                sem, inc=1, device_id=slice_of(tm + distance), device_id_type=MESH
            )

        @pl.when(z >= distance)
        def _():
            pl.semaphore_signal(
                sem, inc=1, device_id=slice_of(tm - distance), device_id_type=MESH
            )

    def callers(distance):
        return jnp.where(z + distance < half, 1, 0) + jnp.where(z >= distance, 1, 0)

    for ex in range(4):
        for ey in range(4):
            if ex or ey:
                pl.semaphore_signal(barrier, inc=1, device_id=tile(ex, ey), device_id_type=MESH)
    tell(barrier, 1)
    pl.semaphore_signal(barrier, inc=1, device_id=slice_of(partner), device_id_type=MESH)
    def rim_copy(src, rims, m, o):
        dx, dy = OFFSETS[o]
        recv = rim_recv0.at[o // 2] if m is None else rim_recv.at[m - 1, o // 4]
        send = rim_send.at[0 if m is None else m]
        return remote(src, rims.at[o ^ 1], send, recv, tile(dx, dy))

    def mom_copy(moms, m, e):
        recv = mom_recv0.at[(e - 1) // 5] if m is None else mom_recv.at[m - 1, GROUP_OF[e // 4]]
        send = mom_send.at[0 if m is None else m]
        return remote(moms.at[0], moms.at[e], send, recv, tile(-(e // 4), -(e % 4)))

    def bytes_of(region, sem):
        return remote(region, region, sem, sem, tile(0, 0))

    loads = [
        pltpu.make_async_copy(src, dst, load_sem.at[i])
        for i, (src, dst) in enumerate(
            ((pos_hbm, pos_ref), (vor_hbm, vor_ref), (cmat_hbm, cmat_ref), (table_hbm, table))
        )
    ]
    for load in loads:
        load.start()
    for load in loads[:2]:
        load.wait()

    for k in range(5):
        lines = [pos_ref[3 * k + c] for c in range(3)] + [vor_ref[3 * k + c] for c in range(3)]
        start_ref[k] = jnp.concatenate(lines + [jnp.zeros_like(lines[0])] * 2, 0)
    pl.semaphore_wait(barrier, n_x * n_y + callers(1))
    for o in range(8):
        rim_copy(start_ref.at[:, 0:6], rim0.at[:, :, 0:6], None, o).start()
    tell(known_sem.at[0], 1)
    pl.semaphore_signal(known_sem.at[0], inc=1, device_id=slice_of(partner), device_id_type=MESH)
    loads[2].wait()
    for k in range(5):
        state = start_ref[k]
        found = mm(cmat_ref[...], chebyshev_terms(state))
        basis[k] = found
        mom0[0, 6 * k : 6 * k + 6] = moments_of(state, found)[0:6]
    mom0[0, 30:32] = jnp.zeros_like(mom0[0, 30:32])
    for e in range(1, 16):
        mom_copy(mom0, None, e).start()
    far_sums[...] = jnp.zeros_like(far_sums)
    for k in range(5):
        state = start_ref[k]
        side = target_side(state)
        if k < 4:
            width = side.shape[1]
            at = 48 * (k % 2)
            sides2[k // 2, at : at + 48, width * (k % 2) : width * (k % 2 + 1)] = side
            sides2[k // 2, at : at + 48, width * (1 - k % 2) : width * (2 - k % 2)] = jnp.zeros_like(side)
        else:
            sides[...] = side
        acch[k], accl[k] = near_sums(side, [(state, 0.0, 0.0)])
    loads[3].wait()

    def around(i, _):
        bytes_of(rim0.at[pl.ds(2 * i, 2), :, 0:6], rim_recv0.at[i]).wait_recv()

        @pl.when(i > 0)
        def _():
            bytes_of(mom0.at[pl.ds(5 * i - 4, 5)], mom_recv0.at[i - 1]).wait_recv()

        @pl.when(i == 2)
        def _():
            pl.semaphore_wait(known_sem.at[0], callers(1) + 1)
            tell(known_sem.at[1], 2)

        scale = choose(i, [0.2, 1.0])
        sources = [(5 * i - 4 + t) * ((i + 3) // 4) for t in range(5)]
        found = [far_dots(mom0[e], table, e) for e in sources]
        for p in range(2):
            far_sums[p] += scale * sum(f[p] for f in found)
        ox, oy = choose(i, [0.0, 1.0]), choose(i, [1.0, 0.0, 1.0, -1.0])

        def both(k):
            return [(rim0[2 * i, k, 0:6], ox, oy), (rim0[2 * i + 1, k, 0:6], -ox, -oy)]

        for k in (0, 2):
            pair = near_sums_of_two(sides2[k // 2], both(k), both(k + 1))
            for n in range(2):
                acch[k + n] += pair[n][0]
                accl[k + n] += pair[n][1]
        high, low = near_sums(sides[...], both(4))
        acch[4] += high
        accl[4] += low
        return 0

    lax.fori_loop(0, 4, around, 0)
    pl.semaphore_wait(known_sem.at[1], callers(2))
    tell(known_sem.at[2], 4)
    for k in range(5):
        state = start_ref[k]
        local = local_rows(
            far_sums[0, 6 * k : 6 * k + 6], far_sums[1, 6 * k : 6 * k + 6]
        )
        if k == 0:
            coarse[...] = gradient_columns(state, acch[k], accl[k], local, basis[k])
        rates[k] = tendency(state, acch[k], accl[k], local, basis[k])

    here = start_ref[0] + slice_step * sum(QUAD[0][j] * rates[j] for j in range(5))
    mine[0] = here
    out_ref[0] = here

    def later(j, m):
        gap_z = j - half
        near_by = jnp.where(z + j < half, jnp.where(j <= 4, 1, 0), jnp.where(gap_z * gap_z <= 9, 1, 0))

        turn = near_by * (2 - lax.rem(j, 2)) + 3 * (1 - near_by)

        @pl.when((tm + j < n_tm) & (turn == m))
        def _():
            remote(
                coarse, coarse_all.at[tm], coarse_send.at[j], coarse_recv.at[tm], slice_of(tm + j)
            ).start()

        return m

    def step(m, _):
        state_ref = mine.at[m - 1, 0:6]
        rims, moms = rim.at[m - 1, :, 0:6], mom.at[m - 1]
        for o in range(8):
            rim_copy(state_ref, rims, m, o).start()
        state = mine[m - 1]
        terms = chebyshev_terms(state)
        moms[0] = moments_of(state, mm(cmat_ref[0:ROWS_MOMENTS], terms))
        sent = mom.at[m - 1, :, 0:6]
        for e in SOURCES:
            mom_copy(sent, m, e).start()
        basis[0, ROWS_MOMENTS:ROWS_ALL] = mm(cmat_ref[ROWS_MOMENTS:ROWS_ALL], terms)
        targets = target_side(state)
        high, low = near_sums(targets, [(state, 0.0, 0.0)])
        acch[0] = high
        accl[0] = low

        def some(first, last):
            tiles = [
                (rim[m - 1, o, 0:6], float(OFFSETS[o][0]), float(OFFSETS[o][1]))
                for o in range(first, last)
            ]
            high, low = near_sums(targets, tiles)
            acch[0] += high
            accl[0] += low

        bytes_of(rim.at[m - 1, 0:4, 0:6], rim_recv.at[m - 1, 0]).wait_recv()
        some(0, 4)
        bytes_of(rim.at[m - 1, 4:8, 0:6], rim_recv.at[m - 1, 1]).wait_recv()
        bytes_of(mom.at[m - 1, 1:8, 0:6], mom_recv.at[m - 1, 0]).wait_recv()
        bytes_of(mom.at[m - 1, 12:16, 0:6], mom_recv.at[m - 1, 2]).wait_recv()
        lax.fori_loop(1, n_tm, later, m)
        far = [far_dots(moms[e], table, e) for e in (*range(8), *range(12, 16))]
        for p in range(2):
            far_sums[p, 0:8] = sum(f[p] for f in far)
        some(4, 8)
        bytes_of(mom.at[m - 1, 8:12, 0:6], mom_recv.at[m - 1, 1]).wait_recv()
        far = [far_dots(moms[e], table, e) for e in range(8, 12)]

        @pl.when(m == 2)
        def _():
            pl.semaphore_wait(known_sem.at[2], callers(4))

            @pl.when(tm > 0)
            def _():
                remote(start_ref.at[0], following, next_send, next_recv, slice_of(tm - 1)).start()


        local = local_rows(*(far_sums[p, 0:8] + sum(f[p] for f in far) for p in range(2)))
        rate = tendency(state, acch[0], accl[0], local, basis[0])
        width = choose(m, [0.0, *(slice_step * WIDTHS[k] for k in (1, 2, 3))])
        total = state
        for j in range(5):
            weight = choose(
                m,
                [0.0]
                + [
                    slice_step * (QUAD[k][j] - (WIDTHS[k] if j == k else 0.0)) for k in (1, 2, 3)
                ],
            )
            total = total + weight * rates[j]
        total = total + width * rate
        mine[m] = total
        out_ref[m] = total
        return 0

    lax.fori_loop(1, 4, step, 0)

    @pl.when(tm < n_tm - 1)
    def _():
        remote(start_ref.at[0], following, next_send, next_recv, slice_of(tm)).wait_recv()
        gap[...] = mine[3] - following[...]

    def gap_copy(j, k, device):
        return remote(
            gap.at[0:6], gap_all.at[k, 0:6], gap_send.at[j], gap_recv.at[k], slice_of(device)
        )

    def send_gap(j, _):
        @pl.when(tm + j < n_tm)
        def _():
            gap_copy(j, tm, tm + j).start()

        return 0

    lax.fori_loop(1, n_tm, send_gap, 0)

    def arrived(k, _):
        @pl.when(k < tm)
        def _():
            remote(coarse, coarse_all.at[k], coarse_send.at[0], coarse_recv.at[k], slice_of(tm)).wait_recv()
            gap_copy(0, k, tm).wait_recv()

        return 0

    lax.fori_loop(0, n_tm - 1, arrived, 0)
    moved = jnp.zeros((3, gap_all.shape[2]), f32)
    spun = jnp.zeros_like(moved)
    for k in range(n_tm - 1):
        g = gap_all[k]
        a = coarse_all[k]
        after = g[3:6] + (a[0:3] * row(spun, 0) + a[3:6] * row(spun, 1) + a[6:9] * row(spun, 2))
        spun = jnp.where(k < tm, after, spun)
        moved = jnp.where(k < tm, moved + g[0:3], moved)
    out_ref[4] = start_ref[0] + jnp.concatenate([moved, spun, jnp.zeros_like(moved[0:2])], 0)

    bytes_of(rim0.at[:, :, 0:6], rim_send.at[0]).wait_send()
    bytes_of(mom0.at[1:16], mom_send.at[0]).wait_send()
    for m in range(1, 4):
        bytes_of(rim.at[m - 1, :, 0:6], rim_send.at[m]).wait_send()
        bytes_of(mom.at[m - 1, 1:16, 0:6], mom_send.at[m]).wait_send()

    @pl.when(tm > 0)
    def _():
        remote(start_ref.at[0], following, next_send, next_recv, slice_of(tm - 1)).wait_send()

    def gone(j, _):
        @pl.when(tm + j < n_tm)
        def _():
            remote(coarse, coarse_all.at[0], coarse_send.at[j], coarse_recv.at[0], slice_of(tm)).wait_send()
            gap_copy(j, 0, tm).wait_send()

        return 0

    lax.fori_loop(1, n_tm, gone, 0)


def spread(all_ref, sp_ref, sv_ref, rp_ref, rv_ref):
    for m in range(4):
        for c in range(3):
            sp_ref[3 * m + c] = all_ref[m, c : c + 1]
            sv_ref[3 * m + c] = all_ref[m, 3 + c : 4 + c]
    for c in range(3):
        rp_ref[c] = all_ref[4, c : c + 1]
        rv_ref[c] = all_ref[4, 3 + c : 4 + c]


def local(cmat, table, positions, vorticity):
    nodes, blobs = positions.shape[1], positions.shape[-1]
    n_tm = lax.axis_size("tm")
    places = positions.reshape(nodes * 3, 1, blobs)
    vortices = vorticity.reshape(nodes * 3, 1, blobs)
    vmem = pl.BlockSpec(memory_space=pltpu.VMEM)
    dma = pltpu.SemaphoreType.DMA
    everything = pl.pallas_call(
        kernel,
        out_shape=jax.ShapeDtypeStruct((5, 8, blobs), f32),
        in_specs=[pl.BlockSpec(memory_space=pl.ANY)] * 4,
        out_specs=vmem,
        scratch_shapes=[
            pltpu.VMEM((nodes * 3, 1, blobs), f32),
            pltpu.VMEM((nodes * 3, 1, blobs), f32),
            pltpu.VMEM(cmat.shape, bf16),
            pltpu.VMEM((5, 8, blobs), f32),
            pltpu.VMEM((32, 80, 512), bf16),
            pltpu.VMEM((8, 5, 8, blobs), f32),
            pltpu.VMEM((3, 8, 8, blobs), f32),
            pltpu.VMEM((4, 8, blobs), f32),
            pltpu.VMEM((16, 32, 128), f32),
            pltpu.VMEM((3, 16, 8, 128), f32),
            pltpu.VMEM((5, ROWS_ALL, blobs), f32),
            pltpu.VMEM((48, blobs), bf16),
            pltpu.VMEM((2, 96, 2 * blobs), bf16),
            pltpu.VMEM((5, 128, blobs), f32),
            pltpu.VMEM((5, 80, blobs), f32),
            pltpu.VMEM((2, 32, 256), f32),
            pltpu.VMEM((5, 8, blobs), f32),
            pltpu.VMEM((9, blobs), f32),
            pltpu.VMEM((n_tm, 9, blobs), f32),
            pltpu.VMEM((8, blobs), f32),
            pltpu.VMEM((n_tm, 8, blobs), f32),
            pltpu.VMEM((8, blobs), f32),
            dma((4,)),
            dma((4,)),
            dma((4,)),
            dma((3, 2)),
            dma((4,)),
            dma((3,)),
            dma((3, 3)),
            dma,
            dma,
            dma((n_tm,)),
            dma((n_tm,)),
            dma((n_tm,)),
            dma((n_tm,)),
            pltpu.SemaphoreType.REGULAR((3,)),
        ],
        compiler_params=pltpu.CompilerParams(collective_id=0, has_side_effects=True),
        name="iteration",
    )(places, vortices, jnp.asarray(cmat), jnp.asarray(table))
    sp, sv, rp, rv = pl.pallas_call(
        spread,
        out_shape=tuple(jax.ShapeDtypeStruct((n, 1, blobs), f32) for n in (12, 12, 3, 3)),
        in_specs=[vmem],
        out_specs=[vmem] * 4,
        name="spread",
    )(everything)
    return (
        sp.reshape(1, 4, 3, 1, 1, blobs),
        sv.reshape(1, 4, 3, 1, 1, blobs),
        rp.reshape(1, 3, 1, 1, blobs),
        rv.reshape(1, 3, 1, 1, blobs),
    )


def solution(mesh):
    return jax.shard_map(
        functools.partial(local, basis_matrix(), far_table()),
        mesh=mesh,
        in_specs=(P("tm", None, None, "tx", "ty", None), P("tm", None, None, "tx", "ty", None)),
        out_specs=(
            P("tm", None, None, "tx", "ty", None),
            P("tm", None, None, "tx", "ty", None),
            P("tm", None, "tx", "ty", None),
            P("tm", None, "tx", "ty", None),
        ),
        check_vma=False,
    )
```
